128 devices in a mesh: row: 8 (over y_lo, z), col: 16 (over x, y_hi, core).
Axes of the slice: x: 4, y: 4 (y_hi: 2, y_lo: 2; y = y_hi * 2 + y_lo), z: 4, core: 2. Of those that a mesh axis runs over, the one named last changes fastest.
Arguments:
- series: bfloat16 [384, 57344], P(None, 'col'), may hold values from -6 to 6
- omega_tiles: float32 [8, 16, 10, 512, 512], P('row', 'col'), may hold values from -3 to 40, as said below
- tile_row: int32 [8, 16, 10], P('row', 'col'), may hold values from 0 to 13, as said below
- tile_col: int32 [8, 16, 10], P('row', 'col'), may hold values from 0 to 6, as said below
- tile_count: int32 [8, 16], P('row', 'col'), may hold values from 1 to 10, as said below
Outputs:
- omega_next: float32 [8, 16, 10, 512, 512], P('row', 'col')
- step_values: float32 [2], replicated
The draws below stay inside these ranges and needn't reach their ends.
Inputs may be any that keep to these rules, and one draw needn't show every extreme that they name: `tile_row`: the live slots of one device name distinct blocks of its band; every block of the band that lies on the matrix's diagonal is among them; slots that are not live hold 0. `tile_col`: as for tile_row. `tile_count`: some device uses all 10 slots in every draw. `omega_tiles`: diagonal entries of the matrix are positive; slots that are not live are zero.
All inputs are finite; a program needn't handle non-finite values.
Results may differ from the reference program's by a relative error of at most 0.0016.
Values may be sent and summed in bfloat16 or wider, within the bound.
A program may use at most 384 MiB of HBM per device.

```python
import jax
import jax.numpy as jnp
from jax import lax

TILE = 512
BLK_DEV = 7
TMAX = 10
SCANS = 384
NBLK = 112
RBLK = 14
VOXELS = 57344
N_ROW = 8
N_COL = 16


def pattern(key):
    base = jax.random.fold_in(key, 7)
    key_load = jax.random.fold_in(base, 1)
    key_full = jax.random.fold_in(base, 2)
    key_rank = jax.random.fold_in(base, 3)
    cells = RBLK * BLK_DEV
    loads = jax.random.randint(key_load, (N_ROW, N_COL), 1, 11)
    extra = jnp.maximum(1, loads * loads * TMAX // 100)
    forced = jax.random.randint(key_full, (), 0, N_ROW * N_COL)
    row_ids = jnp.arange(N_ROW, dtype=jnp.int32)[:, None]
    col_ids = jnp.arange(N_COL, dtype=jnp.int32)[None, :]
    device_id = row_ids * N_COL + col_ids
    cand = jnp.arange(cells, dtype=jnp.int32)
    cand_row = cand // BLK_DEV
    cand_col = cand % BLK_DEV
    is_diag = row_ids[:, :, None] * RBLK + cand_row[None, None, :] == col_ids[:, :, None] * BLK_DEV + cand_col[None, None, :]
    diag_count = jnp.sum(is_diag.astype(jnp.int32), axis=-1)
    counts = jnp.where(device_id == forced, TMAX, jnp.minimum(TMAX, diag_count + extra)).astype(jnp.int32)
    scores = jax.random.randint(key_rank, (N_ROW, N_COL, cells), 0, 2 ** 20) * cells + cand[None, None, :]
    scores = jnp.where(is_diag, cand[None, None, :] - cells, scores)
    ranked = jnp.argsort(scores, axis=-1)[:, :, :TMAX].astype(jnp.int32)
    is_live = jnp.arange(TMAX, dtype=jnp.int32)[None, None, :] < counts[:, :, None]
    local_rows = jnp.where(is_live, ranked // BLK_DEV, 0).astype(jnp.int32)
    local_cols = jnp.where(is_live, ranked % BLK_DEV, 0).astype(jnp.int32)
    return (local_rows, local_cols, counts, is_live)


def draw_tile_row(key, part):
    return pattern(key)[0]


def draw_tile_col(key, part):
    return pattern(key)[1]


def draw_tile_count(key, part):
    return pattern(key)[2]


def draw_omega_tiles(key, part):
    local_rows, local_cols, counts, is_live = pattern(key)
    key_noise = jax.random.fold_in(key, 11)
    key_diag = jax.random.fold_in(key, 12)
    row_ids = jnp.arange(N_ROW, dtype=jnp.int32)[:, None, None]
    col_ids = jnp.arange(N_COL, dtype=jnp.int32)[None, :, None]
    global_rows = row_ids * RBLK + local_rows
    global_cols = col_ids * BLK_DEV + local_cols
    on_diag = jnp.logical_and(is_live, global_rows == global_cols).astype(jnp.float32)
    fraction = global_rows.astype(jnp.float32) / (NBLK - 1)
    noise = 0.05 * jax.random.truncated_normal(key_noise, -6.0, 6.0, (N_ROW, N_COL, TMAX, TILE, TILE), jnp.float32)
    identity = jnp.eye(TILE, dtype=jnp.float32)
    scale = 1.0 + 2.0 * fraction
    diag_vals = jax.random.uniform(key_diag, (N_ROW, N_COL, TMAX, TILE), jnp.float32, 1.0, 2.0)
    tiles = noise + on_diag[..., None, None] * identity * diag_vals[..., None, :]
    tiles = tiles * scale[..., None, None] * is_live.astype(jnp.float32)[..., None, None]
    return tiles.astype(jnp.float32)


def steps_of(key, dims, split, least, largest):
    def one(dim, shards_of):
        heights = jax.random.uniform(jax.random.fold_in(jax.random.fold_in(key, 6), dim), (shards_of,), jnp.float32, least / len(split), largest / len(split))
        return jnp.repeat(jnp.exp(heights), dims[dim] // shards_of).reshape((-1,) + (1,) * (len(dims) - dim - 1))

    gain = one(*split[0])
    for cut in split[1:]:
        gain = gain * one(*cut)
    return gain


def bell_draw(own_key, extent, spread, most, cuts=(), kind=jnp.bfloat16):
    values = jax.random.normal(own_key, extent, jnp.float32) * spread
    if len(cuts) > 0:
        values = steps_of(own_key, extent, cuts, -0.22, 0.18) * values
    return jnp.clip(values, min=-most, max=most).astype(kind)


def setup_inputs(seed: int = 0) -> dict:
    arg_keys = jax.random.split(jax.random.key(seed), 6)
    return {
        "series": bell_draw(arg_keys[0], (SCANS, VOXELS), 1.0, 6.0, ((1, 16),)),
        "omega_tiles": draw_omega_tiles(jax.random.fold_in(arg_keys[5], 71), 0),
        "tile_row": draw_tile_row(jax.random.fold_in(arg_keys[5], 71), 0),
        "tile_col": draw_tile_col(jax.random.fold_in(arg_keys[5], 71), 0),
        "tile_count": draw_tile_count(jax.random.fold_in(arg_keys[5], 71), 0),
    }


step_size = 0.1
penalty = 0.3


def reference(series, omega_tiles, tile_row, tile_col, tile_count):
    band_rows = (jnp.arange(N_ROW, dtype=jnp.int32)[:, None, None] * RBLK + tile_row).reshape(-1).astype(jnp.int32)
    band_cols = (jnp.arange(N_COL, dtype=jnp.int32)[None, :, None] * BLK_DEV + tile_col).reshape(-1).astype(jnp.int32)
    is_live = (jnp.arange(TMAX, dtype=jnp.int32)[None, None, :] < tile_count[:, :, None]).reshape(-1)
    live_float = is_live.astype(jnp.float32)
    flat_tiles = omega_tiles.reshape(-1, TILE, TILE) * live_float[:, None, None]
    panels = series.reshape(SCANS, NBLK, TILE)

    def accumulate(running, position):
        row_acc, col_acc = running
        rounded = flat_tiles[position].astype(jnp.bfloat16)
        right_panel = panels[:, band_cols[position], :]
        left_panel = panels[:, band_rows[position], :]
        row_acc = row_acc.at[band_rows[position]].add(jnp.dot(rounded, right_panel.T, preferred_element_type=jnp.float32))
        col_acc = col_acc.at[band_cols[position]].add(jnp.dot(left_panel, rounded, preferred_element_type=jnp.float32))
        return (row_acc, col_acc), None

    initial = (jnp.zeros((NBLK, TILE, SCANS), jnp.float32), jnp.zeros((NBLK, SCANS, TILE), jnp.float32))
    slots = jnp.arange(flat_tiles.shape[0], dtype=jnp.int32)
    (row_sum, col_sum), unused = lax.scan(accumulate, initial, slots)
    row_half = row_sum.astype(jnp.bfloat16)
    col_half = col_sum.astype(jnp.bfloat16)
    identity = jnp.eye(TILE, dtype=jnp.float32)

    def update(position):
        current = flat_tiles[position]
        rows_at = band_rows[position]
        cols_at = band_cols[position]
        right_panel = panels[:, cols_at, :]
        left_panel = panels[:, rows_at, :]
        gradient = (0.5 / SCANS) * (jnp.dot(row_half[rows_at], right_panel, preferred_element_type=jnp.float32)
                                    + jnp.dot(left_panel.T, col_half[cols_at], preferred_element_type=jnp.float32))
        on_diag = jnp.logical_and(is_live[position], rows_at == cols_at).astype(jnp.float32)
        diag_vals = jnp.diagonal(current)
        safe_diag = jnp.where(on_diag > 0, diag_vals, 1.0)
        gradient = gradient - on_diag * identity * (1.0 / safe_diag)[None, :]
        center = on_diag * identity
        stepped = current - step_size * gradient
        shrunk = jnp.sign(stepped) * jnp.maximum(jnp.abs(stepped) - step_size * penalty, 0.0)
        updated = jnp.where(center > 0, stepped, shrunk) * live_float[position]
        change = updated - current
        partial_terms = jnp.stack([on_diag * jnp.sum(jnp.log(safe_diag)),
                                   jnp.sum(jnp.abs(current) * (1.0 - center)),
                                   jnp.sum(gradient * change),
                                   jnp.sum(change * change),
                                   jnp.sum(jnp.abs(updated) * (1.0 - center))])
        return updated, partial_terms

    updated_tiles, partial_terms = lax.map(update, slots)
    totals = jnp.sum(partial_terms, axis=0)
    squares = jnp.sum(row_sum * row_sum)
    smooth = -totals[0] + squares / (2.0 * SCANS)
    objective = smooth + penalty * totals[1]
    model_bound = smooth + totals[2] + totals[3] / (2.0 * step_size) + penalty * totals[4]
    return updated_tiles.reshape(omega_tiles.shape), jnp.stack([objective, model_bound])
```

```python
import functools

import jax
import jax.numpy as jnp
from jax import lax
from jax.experimental import pallas as pl
from jax.experimental.pallas import tpu as pltpu
from jax.sharding import PartitionSpec as P

MESH = pl.DeviceIdType.MESH
F32 = jnp.float32
BF16 = jnp.bfloat16

STEP = 0.1
PENALTY = 0.3
THRESH = STEP * PENALTY

TILE = 512
BLK = 7
BAND = 14
SLOTS = 10
SCANS = 384

ROWS = BAND * TILE
HALF = ROWS // 2
ROW_LEN = (1152, 1152, 1280)
ROW_BASE = (0, 1152, 2304)
COLS = BLK * SCANS
COL_LEN = (896, 896, 896)
COL_BASE = (0, 896, 1792)
PIECE_BASE = (0, 144, 288)
OWN = HALF // 8
CHUNKS = 14
CH = SCANS // 2


class Place:
    def __init__(self):
        self.row = lax.axis_index("row")
        self.col = lax.axis_index("col")
        self.yl = self.row // 4
        self.z = self.row % 4
        self.x = self.col // 4
        self.yh = (self.col // 2) % 2
        self.core = self.col % 2
        self.bits = {
            "xa": ((self.x + 1) // 2) % 2,
            "xb": self.x // 2,
            "yh": self.yh,
            "za": ((self.z + 1) // 2) % 2,
            "zb": self.z // 2,
            "yl": self.yl,
            "core": self.core,
        }

    def at(self, x=None, yh=None, core=None, yl=None, z=None):
        x = self.x if x is None else x
        yh = self.yh if yh is None else yh
        core = self.core if core is None else core
        yl = self.yl if yl is None else yl
        z = self.z if z is None else z
        return (yl * 4 + z, x * 4 + yh * 2 + core)

    def partner(self, dim):
        if dim == "core":
            return self.at(core=1 - self.core)
        if dim == "yh":
            return self.at(yh=1 - self.yh)
        if dim == "yl":
            return self.at(yl=1 - self.yl)
        if dim == "xa":
            return self.at(x=self.x + 1 - 2 * (self.x % 2))
        if dim == "xb":
            return self.at(x=(self.x + 3 + 2 * (self.x % 2)) % 4)
        if dim == "za":
            return self.at(z=self.z + 1 - 2 * (self.z % 2))
        return self.at(z=(self.z + 3 + 2 * (self.z % 2)) % 4)


ROW_ORDERS = (("xa", "xb", "yh"), ("xb", "yh", "xa"), ("yh", "xa", "xb"))
COL_ORDERS = (("za", "zb", "yl"), ("zb", "yl", "za"), ("yl", "za", "zb"))


def greet(place, dims):
    barrier = pltpu.get_barrier_semaphore()
    for dim in dims:
        pl.semaphore_signal(barrier, inc=1, device_id=place.partner(dim), device_id_type=MESH)
    pl.semaphore_wait(barrier, len(dims))


def segments(place, base, length, dims):
    out = []
    start, n = base, length
    for dim in dims:
        n = n // 2
        bit = place.bits[dim]
        keep = pl.multiple_of(start + bit * n, 16)
        send = pl.multiple_of(start + (1 - bit) * n, 16)
        out.append((keep, send, n))
        start = keep
    return out


def block_of(n):
    for blk in (128, 112, 96, 80, 64, 48, 32, 16):
        if n % blk == 0:
            return blk
    return n


def add_rows(dst, dst_at, one, one_at, two, two_at, n):
    blk = block_of(n)

    def body(i, carry):
        o = i * blk
        a = one[pl.ds(pl.multiple_of(one_at + o, 16), blk), :].astype(F32)
        b = two[pl.ds(pl.multiple_of(two_at + o, 16), blk), :].astype(F32)
        dst[pl.ds(pl.multiple_of(dst_at + o, 16), blk), :] = (a + b).astype(dst.dtype)
        return carry

    lax.fori_loop(0, n // blk, body, 0)


def row_partial_kernel(rows_s, cols_s, meta_s, omega_ref, series_ref, out_ref, acc_ref):
    s = pl.program_id(0)

    @pl.when(s == 0)
    def _():
        def zero(i, carry):
            acc_ref[i] = jnp.zeros((TILE, SCANS), F32)
            return carry

        lax.fori_loop(0, BAND, zero, 0)

    @pl.when(s < meta_s[0])
    def _():
        half = omega_ref[0].astype(BF16)
        at = pl.multiple_of(cols_s[s] * TILE, TILE)
        panel = series_ref[:, pl.ds(at, TILE)]
        term = lax.dot_general(half, panel, (((1,), (1,)), ((), ())), preferred_element_type=F32)
        acc_ref[rows_s[s]] += term

    @pl.when(s == SLOTS - 1)
    def _():
        def cast(i, carry):
            out_ref[i] = acc_ref[i].astype(BF16)
            return carry

        lax.fori_loop(0, BAND, cast, 0)


def col_partial_kernel(rows_s, cols_s, meta_s, omega_ref, band_ref, out_ref, acc_ref):
    s = pl.program_id(0)

    @pl.when(s == 0)
    def _():
        def zero(i, carry):
            acc_ref[i] = jnp.zeros((SCANS, TILE), F32)
            return carry

        lax.fori_loop(0, BLK, zero, 0)

    @pl.when(s < meta_s[0])
    def _():
        half = omega_ref[0].astype(BF16)
        acc_ref[cols_s[s]] += jnp.dot(band_ref[0], half, preferred_element_type=F32)

    @pl.when(s == SLOTS - 1)
    def _():
        def cast(i, carry):
            out_ref[i] = acc_ref[i].astype(BF16)
            return carry

        lax.fori_loop(0, BLK, cast, 0)


def band_kernel(series, part, band, own, squares, sbuf, acc, recv_core, recv_st,
                ss_r, rs_r, ss_b, rs_b, ss_y, ss_s, rs_s, ls):
    place = Place()
    core = place.core
    xs = place.yl * 2 + place.z // 2
    ys = place.z % 2
    sign = 1 - 2 * core
    d = (sign * (place.x - xs) + 4) % 4
    source = jnp.logical_and(d == 0, place.yh == ys)
    follow = jnp.logical_not(source)
    onward = place.at(x=(place.x + sign + 4) % 4)
    sister = place.partner("core")
    across = place.partner("yh")

    greet(place, ("core", "xa", "xb", "yh"))

    keep0 = pl.multiple_of(core * HALF, 16)
    send0 = pl.multiple_of((1 - core) * HALF, 16)
    first = pltpu.make_async_remote_copy(
        part.at[pl.ds(send0, HALF)], recv_core, ss_r.at[9], rs_r.at[9], device_id=sister, device_id_type=MESH)
    first.start()
    mine = pltpu.make_async_copy(part.at[pl.ds(keep0, HALF)], acc, ls.at[0])
    mine.start()

    def slot(i, which):
        return band.at[which * BLK + i // 2, pl.ds((i % 2) * CH, CH), :]

    def native(i):
        return sbuf.at[:, pl.ds((i // 2) * TILE, TILE)].at[pl.ds((i % 2) * CH, CH), :]

    def to_next(src, i):
        return pltpu.make_async_remote_copy(src, slot(i, core), ss_b.at[i], rs_b.at[i],
                                            device_id=onward, device_id_type=MESH)

    def to_across(src, i):
        return pltpu.make_async_remote_copy(src, slot(i, core), ss_y.at[i], rs_b.at[i],
                                            device_id=across, device_id_type=MESH)

    def to_sister(src, i):
        return pltpu.make_async_remote_copy(src, slot(i, core), ss_s.at[i], rs_s.at[i],
                                            device_id=sister, device_id_type=MESH)

    def keep_native(i):
        return pltpu.make_async_copy(native(i), slot(i, core), ls.at[2 + i])

    load = pltpu.make_async_copy(series, sbuf, ls.at[1])

    @pl.when(source)
    def _():
        load.start()
        load.wait()

    def source_step(i):
        @pl.when(source)
        def _():
            to_next(native(i), i).start()
            to_across(native(i), i).start()
            to_sister(native(i), i).start()
            keep_native(i).start()

    def follow_step(i):
        @pl.when(follow)
        def _():
            to_next(slot(i, core), i).wait_recv()

            @pl.when(d < 3)
            def _():
                to_next(slot(i, core), i).start()

            to_sister(slot(i, core), i).start()

    segs = [segments(place, ROW_BASE[o], ROW_LEN[o], ROW_ORDERS[o]) for o in range(3)]
    recv_at = []
    at = 0
    for o in range(3):
        line = []
        for keep, send, n in segs[o]:
            line.append(at)
            at += n
        recv_at.append(line)

    def exchange(o, j):
        keep, send, n = segs[o][j]
        return pltpu.make_async_remote_copy(
            acc.at[pl.ds(send, n)], recv_st.at[pl.ds(recv_at[o][j], n)], ss_r.at[o * 3 + j], rs_r.at[o * 3 + j],
            device_id=place.partner(ROW_ORDERS[o][j]), device_id_type=MESH)

    source_step(0)
    source_step(1)
    mine.wait()
    first.wait_recv()
    add_rows(acc, 0, acc, 0, recv_core, 0, HALF)
    for o in range(3):
        exchange(o, 0).start()
    for i in range(0, 4):
        source_step(i + 2)
        follow_step(i)
    for o in range(3):
        keep, send, n = segs[o][0]
        exchange(o, 0).wait_recv()
        add_rows(acc, keep, acc, keep, recv_st, recv_at[o][0], n)
        exchange(o, 1).start()
    for i in range(4, 8):
        source_step(i + 2)
        follow_step(i)
    for o in range(3):
        keep, send, n = segs[o][1]
        exchange(o, 1).wait_recv()
        add_rows(acc, keep, acc, keep, recv_st, recv_at[o][1], n)
        exchange(o, 2).start()
    for i in range(8, CHUNKS):
        if i + 2 < CHUNKS:
            source_step(i + 2)
        follow_step(i)
    total = jnp.zeros((8, SCANS), F32)
    for o in range(3):
        keep, send, n = segs[o][2]
        exchange(o, 2).wait_recv()

        def body(i, total, o=o, keep=keep):
            a = acc[pl.ds(pl.multiple_of(keep + i * 16, 16), 16), :].astype(F32)
            b = recv_st[pl.ds(pl.multiple_of(recv_at[o][2] + i * 16, 16), 16), :].astype(F32)
            c = a + b
            own[pl.ds(pl.multiple_of(PIECE_BASE[o] + i * 16, 16), 16), :] = c.astype(BF16)
            c2 = c * c
            return total + c2[:8] + c2[8:]

        total = lax.fori_loop(0, n // 16, body, total)
    squares[...] = total
    for i in range(CHUNKS):
        to_sister(slot(i, 1 - core), i).wait_recv()
        to_sister(slot(i, core), i).wait_send()

        @pl.when(d < 3)
        def _():
            to_next(slot(i, core), i).wait_send()

        @pl.when(source)
        def _():
            to_across(native(i), i).wait_send()
            keep_native(i).wait()
    first.wait_send()
    for o in range(3):
        for j in range(3):
            exchange(o, j).wait_send()


def sums_kernel(own, colpart, rowhalf, colhalf, acc, recv, fin, ss_r, rs_r, ss_s, rs_s, ss_c, rs_c, ls):
    place = Place()
    core = place.core
    sister = place.partner("core")
    greet(place, ("core", "xa", "xb", "yh", "za", "zb", "yl"))

    csegs = [segments(place, COL_BASE[o], COL_LEN[o], COL_ORDERS[o]) for o in range(3)]
    recv_at = []
    at = 0
    for o in range(3):
        line = []
        for keep, send, n in csegs[o]:
            line.append(at)
            at += n
        recv_at.append(line)

    def exchange(o, j):
        keep, send, n = csegs[o][j]
        src = colpart if j == 0 else acc
        return pltpu.make_async_remote_copy(
            src.at[pl.ds(send, n)], recv.at[pl.ds(recv_at[o][j], n)], ss_c.at[o * 6 + j], rs_c.at[o * 6 + j],
            device_id=place.partner(COL_ORDERS[o][j]), device_id_type=MESH)

    rsegs = [segments(place, ROW_BASE[o], ROW_LEN[o], ROW_ORDERS[o]) for o in range(3)]
    home = core * HALF
    away = (1 - core) * HALF

    def row_at(which, start, n):
        return rowhalf.at[pl.ds(pl.multiple_of(which + start, 16), n)]

    def row_gather(o, j):
        keep, send, n = rsegs[o][j]
        src = own.at[pl.ds(PIECE_BASE[o], n)] if j == 2 else row_at(home, keep, n)
        return pltpu.make_async_remote_copy(
            src, row_at(home, keep, n), ss_r.at[o * 3 + j], rs_r.at[o * 3 + j],
            device_id=place.partner(ROW_ORDERS[o][j]), device_id_type=MESH)

    def row_arrived(o, j):
        keep, send, n = rsegs[o][j]
        return pltpu.make_async_remote_copy(
            row_at(home, send, n), row_at(home, send, n), ss_r.at[o * 3 + j], rs_r.at[o * 3 + j],
            device_id=place.partner(ROW_ORDERS[o][j]), device_id_type=MESH)

    def row_local(o):
        keep, send, n = rsegs[o][2]
        return pltpu.make_async_copy(own.at[pl.ds(PIECE_BASE[o], n)], row_at(home, keep, n), ls.at[o])

    def row_share(o, j, which=None):
        if j == 3:
            keep, send, n = rsegs[o][2]
            src = own.at[pl.ds(PIECE_BASE[o], n)]
            start = keep
        else:
            keep, send, n = rsegs[o][j]
            src = row_at(home, send, n)
            start = send
        return pltpu.make_async_remote_copy(
            src, row_at(home, start, n), ss_s.at[o * 4 + j], rs_s.at[o * 4 + j], device_id=sister, device_id_type=MESH)

    def col_at(start, n):
        return colhalf.at[pl.ds(start, n)]

    def col_gather(o, j):
        keep, send, n = csegs[o][j]
        src = fin.at[pl.ds(o * 112, n)] if j == 2 else col_at(keep, n)
        return pltpu.make_async_remote_copy(
            src, col_at(keep, n), ss_c.at[o * 6 + 3 + j], rs_c.at[o * 6 + 3 + j],
            device_id=place.partner(COL_ORDERS[o][j]), device_id_type=MESH)

    def col_local(o):
        keep, send, n = csegs[o][2]
        return pltpu.make_async_copy(fin.at[pl.ds(o * 112, n)], col_at(keep, n), ls.at[3 + o])

    for o in range(3):
        exchange(o, 0).start()
    for o in range(3):
        row_gather(o, 2).start()
        row_local(o).start()
        row_share(o, 3).start()
    for o in range(3):
        keep, send, n = csegs[o][0]
        exchange(o, 0).wait_recv()
        add_rows(acc, keep, colpart, keep, recv, recv_at[o][0], n)
        exchange(o, 1).start()
    for o in range(3):
        row_local(o).wait()
        row_arrived(o, 2).wait_recv()
        row_gather(o, 1).start()
        row_share(o, 2).start()
    for o in range(3):
        keep, send, n = csegs[o][1]
        exchange(o, 1).wait_recv()
        add_rows(acc, keep, acc, keep, recv, recv_at[o][1], n)
        exchange(o, 2).start()
    for o in range(3):
        keep, send, n = csegs[o][2]
        exchange(o, 2).wait_recv()
        add_rows(fin, o * 112, acc, keep, recv, recv_at[o][2], n)
        col_gather(o, 2).start()
        col_local(o).start()
    for o in range(3):
        row_arrived(o, 1).wait_recv()
        row_gather(o, 0).start()
        row_share(o, 1).start()
    for j in (2, 1):
        for o in range(3):
            if j == 2:
                col_local(o).wait()
            col_gather(o, j).wait_recv()
            col_gather(o, j - 1).start()
    for o in range(3):
        row_arrived(o, 0).wait_recv()
        row_share(o, 0).start()
    for o in range(3):
        col_gather(o, 0).wait_recv()
    for o in range(3):
        for j in range(4):
            row_share(o, j).wait_recv()
            row_share(o, j).wait_send()
        for j in range(3):
            row_gather(o, j).wait_send()
            exchange(o, j).wait_send()
            col_gather(o, j).wait_send()


def update_kernel(rows_s, cols_s, meta_s, omega_ref, rowhalf_ref, band_ref, series_ref, colhalf_ref,
                  out_ref, sums_ref, grad_ref, acc_ref, diag_ref):
    s = pl.program_id(0)
    live = s < meta_s[0]

    @pl.when(s == 0)
    def _():
        acc_ref[...] = jnp.zeros_like(acc_ref)
        diag_ref[...] = jnp.zeros_like(diag_ref)

    @pl.when(jnp.logical_not(live))
    def _():
        out_ref[0] = jnp.zeros((TILE, TILE), F32)

    @pl.when(live)
    def _():
        grad_ref[...] = (0.5 / SCANS) * (
            jnp.dot(rowhalf_ref[0], series_ref[...], preferred_element_type=F32)
            + lax.dot_general(band_ref[0], colhalf_ref[0], (((0,), (0,)), ((), ())), preferred_element_type=F32)
        )
        blk = 32

        def fold(v):
            return v[0:8] + v[8:16] + v[16:24] + v[24:32]

        def body(i, carry):
            before, inner, moved, after = carry
            at = pl.ds(pl.multiple_of(i * blk, blk), blk)
            now = omega_ref[0, at, :]
            grad = grad_ref[at, :]
            stepped = now - STEP * grad
            updated = stepped - jnp.clip(stepped, -THRESH, THRESH)
            change = updated - now
            out_ref[0, at, :] = updated
            return (before + fold(jnp.abs(now)), inner + fold(grad * change), moved + fold(change * change),
                    after + fold(jnp.abs(updated)))

        zero = jnp.zeros((8, TILE), F32)
        before, inner, moved, after = lax.fori_loop(0, TILE // blk, body, (zero, zero, zero, zero))
        acc_ref[0] += before
        acc_ref[1] += inner
        acc_ref[2] += moved
        acc_ref[3] += after

        @pl.when(meta_s[1] + rows_s[s] == meta_s[2] + cols_s[s])
        def _():
            mask = lax.broadcasted_iota(jnp.int32, (128, 128), 0) == lax.broadcasted_iota(jnp.int32, (128, 128), 1)
            for q in range(TILE // 128):
                at = slice(q * 128, (q + 1) * 128)

                def pick(v):
                    return jnp.sum(jnp.where(mask, v, 0.0), axis=0, keepdims=True)

                now = pick(omega_ref[0, at, at])
                plain = pick(grad_ref[at, at])
                shrunk = out_ref[0, at, at]
                old = pick(shrunk)
                grad = plain - 1.0 / now
                stepped = now - STEP * grad
                change = stepped - now
                old_change = old - now
                out_ref[0, at, at] = jnp.where(mask, stepped, shrunk)
                diag_ref[0:1] += jnp.log(now)
                diag_ref[1:2] -= jnp.abs(now)
                diag_ref[2:3] += grad * change - plain * old_change
                diag_ref[3:4] += change * change - old_change * old_change
                diag_ref[4:5] -= jnp.abs(old)

    @pl.when(s == SLOTS - 1)
    def _():
        sums_ref[0:1] = diag_ref[0:1]
        for t in range(4):
            v = acc_ref[t]
            v = v[:, 0:128] + v[:, 128:256] + v[:, 256:384] + v[:, 384:512]
            sums_ref[1 + t:2 + t] = jnp.sum(v, axis=0, keepdims=True) + diag_ref[1 + t:2 + t]
        sums_ref[5:8] = jnp.zeros((3, 128), F32)


def total_kernel(sums, squares, out, vec, recv_a, recv_b, ss, rs):
    place = Place()
    row, col = place.row, place.col
    barrier = pltpu.get_barrier_semaphore()
    for k in range(1, 16):
        pl.semaphore_signal(barrier, inc=1, device_id=(row, (col + k) % 16), device_id_type=MESH)
    for k in range(1, 8):
        pl.semaphore_signal(barrier, inc=1, device_id=((row + k) % 8, col), device_id_type=MESH)
    v = squares[...]
    v = jnp.sum(v, axis=0, keepdims=True)
    v = v[:, 0:128] + v[:, 128:256] + v[:, 256:384]
    spot = lax.broadcasted_iota(jnp.int32, (8, 128), 0) == 5
    vec[0] = sums[...] + jnp.where(spot, jnp.broadcast_to(v, (8, 128)), 0.0)
    pl.semaphore_wait(barrier, 22)

    def across(k):
        return pltpu.make_async_remote_copy(vec.at[0], recv_a.at[col], ss.at[k - 1], rs.at[k - 1],
                                            device_id=(row, (col + k) % 16), device_id_type=MESH)

    def down(k):
        return pltpu.make_async_remote_copy(vec.at[1], recv_b.at[row], ss.at[14 + k], rs.at[14 + k],
                                            device_id=((row + k) % 8, col), device_id_type=MESH)

    for k in range(1, 16):
        across(k).start()
    recv_a[col] = vec[0]
    for k in range(1, 16):
        across(k).wait_recv()
    total = recv_a[0]
    for k in range(1, 16):
        total = total + recv_a[k]
    vec[1] = total
    for k in range(1, 8):
        down(k).start()
    recv_b[row] = total
    for k in range(1, 8):
        down(k).wait_recv()
    total = recv_b[0]
    for k in range(1, 8):
        total = total + recv_b[k]
    s = jnp.sum(total, axis=1, keepdims=True)
    smooth = -s[0:1] + s[5:6] / (2.0 * SCANS)
    objective = smooth + PENALTY * s[1:2]
    bound = smooth + s[2:3] + s[3:4] / (2.0 * STEP) + PENALTY * s[4:5]
    lane = lax.broadcasted_iota(jnp.int32, (1, 128), 1)
    out[...] = jnp.where(lane == 0, objective, bound)
    for k in range(1, 16):
        across(k).wait_send()
    for k in range(1, 8):
        down(k).wait_send()


def local(series, omega_tiles, tile_row, tile_col, tile_count):
    omega = omega_tiles[0, 0]
    rows_s = tile_row[0, 0]
    cols_s = tile_col[0, 0]
    meta = jnp.stack([tile_count[0, 0], lax.axis_index("row") * BAND, lax.axis_index("col") * BLK]).astype(jnp.int32)
    big = 60 << 20
    vmem = pl.BlockSpec(memory_space=pltpu.VMEM)
    hbm = pl.BlockSpec(memory_space=pl.ANY)

    def plain(**kw):
        return pltpu.CompilerParams(vmem_limit_bytes=big, **kw)

    row_part = pl.pallas_call(
        row_partial_kernel,
        out_shape=jax.ShapeDtypeStruct((BAND, TILE, SCANS), BF16),
        grid_spec=pltpu.PrefetchScalarGridSpec(
            num_scalar_prefetch=3, grid=(SLOTS,),
            in_specs=[pl.BlockSpec((1, TILE, TILE), lambda s, *_: (s, 0, 0)),
                      pl.BlockSpec((SCANS, BLK * TILE), lambda s, *_: (0, 0))],
            out_specs=pl.BlockSpec((BAND, TILE, SCANS), lambda s, *_: (0, 0, 0)),
            scratch_shapes=[pltpu.VMEM((BAND, TILE, SCANS), F32)]),
        compiler_params=plain(), name="row_partial",
    )(rows_s, cols_s, meta, omega, series)

    band, own, squares = pl.pallas_call(
        band_kernel,
        out_shape=(jax.ShapeDtypeStruct((BAND, SCANS, TILE), BF16),
                   jax.ShapeDtypeStruct((OWN, SCANS), BF16),
                   jax.ShapeDtypeStruct((8, SCANS), F32)),
        in_specs=[hbm, hbm], out_specs=(hbm, vmem, vmem),
        scratch_shapes=[pltpu.VMEM((SCANS, BLK * TILE), BF16), pltpu.VMEM((HALF, SCANS), BF16),
                        pltpu.VMEM((HALF, SCANS), BF16), pltpu.VMEM((HALF * 7 // 8, SCANS), BF16),
                        pltpu.SemaphoreType.DMA((10,)), pltpu.SemaphoreType.DMA((10,)),
                        pltpu.SemaphoreType.DMA((CHUNKS,)), pltpu.SemaphoreType.DMA((CHUNKS,)),
                        pltpu.SemaphoreType.DMA((CHUNKS,)),
                        pltpu.SemaphoreType.DMA((CHUNKS,)), pltpu.SemaphoreType.DMA((CHUNKS,)),
                        pltpu.SemaphoreType.DMA((CHUNKS + 2,))],
        compiler_params=plain(collective_id=0, has_side_effects=True), name="band",
    )(series, row_part.reshape(ROWS, SCANS))

    col_part = pl.pallas_call(
        col_partial_kernel,
        out_shape=jax.ShapeDtypeStruct((BLK, SCANS, TILE), BF16),
        grid_spec=pltpu.PrefetchScalarGridSpec(
            num_scalar_prefetch=3, grid=(SLOTS,),
            in_specs=[pl.BlockSpec((1, TILE, TILE), lambda s, *_: (s, 0, 0)),
                      pl.BlockSpec((1, SCANS, TILE), lambda s, r, c, m: (r[s], 0, 0))],
            out_specs=pl.BlockSpec((BLK, SCANS, TILE), lambda s, *_: (0, 0, 0)),
            scratch_shapes=[pltpu.VMEM((BLK, SCANS, TILE), F32)]),
        compiler_params=plain(), name="col_partial",
    )(rows_s, cols_s, meta, omega, band)

    row_half, col_half = pl.pallas_call(
        sums_kernel,
        out_shape=(jax.ShapeDtypeStruct((ROWS, SCANS), BF16), jax.ShapeDtypeStruct((COLS, TILE), BF16)),
        in_specs=[vmem, vmem], out_specs=(hbm, hbm),
        scratch_shapes=[pltpu.VMEM((COLS, TILE), BF16), pltpu.VMEM((COLS * 7 // 8, TILE), BF16),
                        pltpu.VMEM((COLS // 8, TILE), BF16),
                        pltpu.SemaphoreType.DMA((9,)), pltpu.SemaphoreType.DMA((9,)),
                        pltpu.SemaphoreType.DMA((12,)), pltpu.SemaphoreType.DMA((12,)),
                        pltpu.SemaphoreType.DMA((18,)), pltpu.SemaphoreType.DMA((18,)),
                        pltpu.SemaphoreType.DMA((6,))],
        compiler_params=plain(collective_id=1, has_side_effects=True), name="sums",
    )(own, col_part.reshape(COLS, TILE))

    omega_next, sums = pl.pallas_call(
        update_kernel,
        out_shape=(jax.ShapeDtypeStruct((SLOTS, TILE, TILE), F32), jax.ShapeDtypeStruct((8, 128), F32)),
        grid_spec=pltpu.PrefetchScalarGridSpec(
            num_scalar_prefetch=3, grid=(SLOTS,),
            in_specs=[pl.BlockSpec((1, TILE, TILE), lambda s, *_: (s, 0, 0)),
                      pl.BlockSpec((1, TILE, SCANS), lambda s, r, c, m: (r[s], 0, 0)),
                      pl.BlockSpec((1, SCANS, TILE), lambda s, r, c, m: (r[s], 0, 0)),
                      pl.BlockSpec((SCANS, TILE), lambda s, r, c, m: (0, c[s])),
                      pl.BlockSpec((1, SCANS, TILE), lambda s, r, c, m: (c[s], 0, 0))],
            out_specs=(pl.BlockSpec((1, TILE, TILE), lambda s, *_: (s, 0, 0)),
                       pl.BlockSpec((8, 128), lambda s, *_: (0, 0))),
            scratch_shapes=[pltpu.VMEM((TILE, TILE), F32), pltpu.VMEM((4, 8, TILE), F32), pltpu.VMEM((8, 128), F32)]),
        compiler_params=plain(), name="update",
    )(rows_s, cols_s, meta, omega, row_half.reshape(BAND, TILE, SCANS), band, series, col_half.reshape(BLK, SCANS, TILE))

    values = pl.pallas_call(
        total_kernel,
        out_shape=jax.ShapeDtypeStruct((1, 128), F32),
        in_specs=[vmem, vmem], out_specs=vmem,
        scratch_shapes=[pltpu.VMEM((2, 8, 128), F32), pltpu.VMEM((16, 8, 128), F32), pltpu.VMEM((8, 8, 128), F32),
                        pltpu.SemaphoreType.DMA((22,)), pltpu.SemaphoreType.DMA((22,))],
        compiler_params=plain(collective_id=2, has_side_effects=True), name="total",
    )(sums, squares)
    return omega_next[None, None], values[0, :2]


def solution(mesh):
    placed = (
        P(None, "col"),
        P("row", "col", None, None, None),
        P("row", "col", None),
        P("row", "col", None),
        P("row", "col"),
    )
    return jax.shard_map(
        local,
        mesh=mesh,
        in_specs=placed,
        out_specs=(P("row", "col", None, None, None), P()),
        check_vma=False,
    )
```

```python
import functools

import jax
import jax.numpy as jnp
from jax import lax
from jax.experimental import pallas as pl
from jax.experimental.pallas import tpu as pltpu
from jax.sharding import PartitionSpec as P

MESH = pl.DeviceIdType.MESH
F32 = jnp.float32
BF16 = jnp.bfloat16

STEP = 0.1
PENALTY = 0.3
THRESH = STEP * PENALTY

TILE = 512
BLK = 7
BAND = 14
SLOTS = 10
SCANS = 384

ROWS = BAND * TILE
HALF = ROWS // 2
ROW_LEN = (1152, 1152, 1280)
COLS = BLK * SCANS
COL_LEN = (640, 640, 640, 768)
SPLIT = 4
CHUNKS = BLK * SPLIT
CH = SCANS // SPLIT


def bases(lengths):
    out, at = [], 0
    for n in lengths:
        out.append(at)
        at += n
    return out


ROW_BASE = bases(ROW_LEN)
COL_BASE = bases(COL_LEN)
ROW_FIN = bases([n // 8 for n in ROW_LEN])
COL_FIN = bases([n // 8 for n in COL_LEN])
RCH = len(ROW_LEN)
CCH = len(COL_LEN)


class Place:
    def __init__(self):
        self.row = lax.axis_index("row")
        self.col = lax.axis_index("col")
        self.yl = self.row // 4
        self.z = self.row % 4
        self.x = self.col // 4
        self.yh = (self.col // 2) % 2
        self.core = self.col % 2
        self.bits = {
            "xa": ((self.x + 1) // 2) % 2,
            "xb": self.x // 2,
            "yh": self.yh,
            "za": ((self.z + 1) // 2) % 2,
            "zb": self.z // 2,
            "yl": self.yl,
            "core": self.core,
        }

    def at(self, x=None, yh=None, core=None, yl=None, z=None):
        x = self.x if x is None else x
        yh = self.yh if yh is None else yh
        core = self.core if core is None else core
        yl = self.yl if yl is None else yl
        z = self.z if z is None else z
        return (yl * 4 + z, x * 4 + yh * 2 + core)

    def partner(self, dim):
        if dim == "core":
            return self.at(core=1 - self.core)
        if dim == "yh":
            return self.at(yh=1 - self.yh)
        if dim == "yl":
            return self.at(yl=1 - self.yl)
        if dim == "xa":
            return self.at(x=self.x + 1 - 2 * (self.x % 2))
        if dim == "xb":
            return self.at(x=(self.x + 3 + 2 * (self.x % 2)) % 4)
        if dim == "za":
            return self.at(z=self.z + 1 - 2 * (self.z % 2))
        return self.at(z=(self.z + 3 + 2 * (self.z % 2)) % 4)


ROW_ORDERS = (("xa", "xb", "yh"), ("xb", "yh", "xa"), ("yh", "xa", "xb"))
COL_ORDERS = (("za", "zb", "yl"), ("zb", "za", "yl"), ("za", "zb", "yl"), ("zb", "za", "yl"))


def greet(place, dims):
    barrier = pltpu.get_barrier_semaphore()
    for dim in dims:
        pl.semaphore_signal(barrier, inc=1, device_id=place.partner(dim), device_id_type=MESH)
    pl.semaphore_wait(barrier, len(dims))


def segments(place, base, length, dims):
    out = []
    start, n = base, length
    for dim in dims:
        n = n // 2
        bit = place.bits[dim]
        keep = pl.multiple_of(start + bit * n, 16)
        send = pl.multiple_of(start + (1 - bit) * n, 16)
        out.append((keep, send, n))
        start = keep
    return out


def block_of(n):
    for blk in (128, 112, 96, 80, 64, 48, 32, 16):
        if n % blk == 0:
            return blk
    return n


def add_rows(dst, dst_at, one, one_at, two, two_at, n):
    blk = block_of(n)

    def body(i, carry):
        o = i * blk
        a = one[pl.ds(pl.multiple_of(one_at + o, 16), blk), :].astype(F32)
        b = two[pl.ds(pl.multiple_of(two_at + o, 16), blk), :].astype(F32)
        dst[pl.ds(pl.multiple_of(dst_at + o, 16), blk), :] = (a + b).astype(dst.dtype)
        return carry

    lax.fori_loop(0, n // blk, body, 0)


def partial_kernel(rows_s, cols_s, count_s, omega_ref, series_ref, band_ref, row_ref, col_ref, racc_ref, cacc_ref):
    s = pl.program_id(0)
    count = count_s[0]

    def again(ids, t):
        seen = False
        for k in range(SLOTS - 1):
            seen = jnp.logical_or(seen, jnp.logical_and(k < t, ids[k] == ids[t]))
        return seen

    @pl.when(s < count)
    def _():
        half = omega_ref[0].astype(BF16)
        at = pl.multiple_of(cols_s[s] * TILE, TILE)
        panel = series_ref[:, pl.ds(at, TILE)]
        row_again = again(rows_s, s)
        col_again = again(cols_s, s)
        term = lax.dot_general(half, panel, (((1,), (1,)), ((), ())), preferred_element_type=F32)

        @pl.when(row_again)
        def _():
            racc_ref[rows_s[s]] += term

        @pl.when(jnp.logical_not(row_again))
        def _():
            racc_ref[rows_s[s]] = term

        term2 = jnp.dot(band_ref[0], half, preferred_element_type=F32)

        @pl.when(col_again)
        def _():
            cacc_ref[cols_s[s]] += term2

        @pl.when(jnp.logical_not(col_again))
        def _():
            cacc_ref[cols_s[s]] = term2

    @pl.when(s == SLOTS - 1)
    def _():
        def finish(ids, acc_ref, out_ref, blocks):
            def one(i, carry):
                held = False
                for k in range(SLOTS):
                    held = jnp.logical_or(held, jnp.logical_and(k < count, ids[k] == i))

                @pl.when(held)
                def _():
                    out_ref[i] = acc_ref[i].astype(BF16)

                @pl.when(jnp.logical_not(held))
                def _():
                    out_ref[i] = jnp.zeros(out_ref.shape[1:], BF16)

                return carry

            lax.fori_loop(0, blocks, one, 0)

        finish(rows_s, racc_ref, row_ref, BAND)
        finish(cols_s, cacc_ref, col_ref, BLK)


def band_kernel(series, band, sbuf, ss_b, rs_b, ss_y, ss_s, rs_s, ls):
    place = Place()
    core = place.core
    xs = place.yl * 2 + place.z // 2
    near = place.yh == place.z % 2
    source = jnp.logical_and(place.x == xs, near)
    sister = place.partner("core")
    over = place.partner("yh")
    dist = [(place.x - xs + 4) % 4, (xs - place.x + 4) % 4]
    onward = [place.at(x=(place.x + 1) % 4), place.at(x=(place.x + 3) % 4)]
    hops = [jnp.where(near, dist[s % 2], (dist[s % 2] + 4 - s // 2) % 4) for s in range(4)]
    lag = [jnp.where(near, 0, s // 2 + 1) + hops[s] for s in range(4)]
    crossing = [jnp.logical_and(near, dist[s % 2] == s // 2) for s in range(4)]

    def slot(i, which):
        return band.at[which * BLK + i // SPLIT, pl.ds(pl.multiple_of((i % SPLIT) * CH, 16), CH), :]

    def native(i):
        return sbuf.at[pl.ds(pl.multiple_of((i % SPLIT) * CH, 16), CH),
                       pl.ds(pl.multiple_of((i // SPLIT) * TILE, TILE), TILE)]

    def to_next(src, i, s):
        return pltpu.make_async_remote_copy(src, slot(i, core), ss_b.at[i], rs_b.at[i],
                                            device_id=onward[s % 2], device_id_type=MESH)

    def to_over(src, i):
        return pltpu.make_async_remote_copy(src, slot(i, core), ss_y.at[i], rs_b.at[i],
                                            device_id=over, device_id_type=MESH)

    def to_sister(src, i):
        return pltpu.make_async_remote_copy(src, slot(i, core), ss_s.at[i], rs_s.at[i],
                                            device_id=sister, device_id_type=MESH)

    def keep_native(i):
        return pltpu.make_async_copy(native(i), slot(i, core), ls.at[1 + i])

    load = pltpu.make_async_copy(series, sbuf, ls.at[0])

    @pl.when(source)
    def _():
        load.start()

    greet(place, ("core", "xa", "xb", "yh"))

    def forward(src, i, s):
        @pl.when(hops[s] < 3)
        def _():
            to_next(src, i, s).start()

        @pl.when(crossing[s])
        def _():
            to_over(src, i).start()

        to_sister(src, i).start()

    @pl.when(source)
    def _():
        load.wait()

        def emit(k, carry):
            for s in range(4):
                i = k * 4 + s
                forward(native(i), i, s)
                keep_native(i).start()
            return carry

        lax.fori_loop(0, CHUNKS // 4, emit, 0)

    @pl.when(jnp.logical_not(source))
    def _():
        def tick(t, carry):
            for s in range(4):
                k = t - lag[s]

                @pl.when(jnp.logical_and(k >= 0, k < CHUNKS // 4))
                def _():
                    i = k * 4 + s
                    to_next(slot(i, core), i, s).wait_recv()
                    forward(slot(i, core), i, s)

            return carry

        lax.fori_loop(0, CHUNKS // 4 + 5, tick, 0)

    def drain(k, carry):
        for s in range(4):
            i = k * 4 + s
            to_sister(slot(i, 1 - core), i).wait_recv()
            to_sister(slot(i, core), i).wait_send()

            @pl.when(hops[s] < 3)
            def _():
                to_next(slot(i, core), i, s).wait_send()

            @pl.when(crossing[s])
            def _():
                to_over(slot(i, core), i).wait_send()

            @pl.when(source)
            def _():
                keep_native(i).wait()

        return carry

    lax.fori_loop(0, CHUNKS // 4, drain, 0)


def sums_kernel(rowpart, colpart, rowhalf, colhalf, squares, racc, rcore, rrecv, rfin, cacc, crecv, cfin,
                ss_k, rs_k, ss_r, rs_r, ss_s, rs_s, ss_c, rs_c, ls):
    place = Place()
    core = place.core
    sister = place.partner("core")
    home = core * HALF
    away = (1 - core) * HALF

    rsegs = [segments(place, ROW_BASE[o], ROW_LEN[o], ROW_ORDERS[o]) for o in range(RCH)]
    csegs = [segments(place, COL_BASE[o], COL_LEN[o], COL_ORDERS[o]) for o in range(CCH)]

    def landing(segs):
        out, at = [], 0
        for line in segs:
            row = []
            for keep, send, n in line:
                row.append(at)
                at += n
            out.append(row)
        return out

    rland = landing(rsegs)
    cland = landing(csegs)

    def part_at(which, o):
        return rowpart.at[pl.ds(pl.multiple_of(which + ROW_BASE[o], 16), ROW_LEN[o])]

    def pair(o):
        at = pl.ds(ROW_BASE[o], ROW_LEN[o])
        return pltpu.make_async_remote_copy(part_at(away, o), rcore.at[at], ss_k.at[o], rs_k.at[o],
                                            device_id=sister, device_id_type=MESH)

    def row_load(o):
        at = pl.ds(ROW_BASE[o], ROW_LEN[o])
        return pltpu.make_async_copy(part_at(home, o), racc.at[at], ls.at[o])

    def col_load(o):
        keep, send, n = csegs[o][0]
        return pltpu.make_async_copy(colpart.at[pl.ds(keep, n)], cacc.at[pl.ds(keep, n)], ls.at[RCH + o])

    def row_send(o, j):
        keep, send, n = rsegs[o][j]
        return pltpu.make_async_remote_copy(
            racc.at[pl.ds(send, n)], rrecv.at[pl.ds(rland[o][j], n)], ss_r.at[o * 6 + j], rs_r.at[o * 6 + j],
            device_id=place.partner(ROW_ORDERS[o][j]), device_id_type=MESH)

    def col_send(o, j):
        keep, send, n = csegs[o][j]
        src = colpart if j == 0 else cacc
        return pltpu.make_async_remote_copy(
            src.at[pl.ds(send, n)], crecv.at[pl.ds(cland[o][j], n)], ss_c.at[o * 6 + j], rs_c.at[o * 6 + j],
            device_id=place.partner(COL_ORDERS[o][j]), device_id_type=MESH)

    def row_at(start, n):
        return rowhalf.at[pl.ds(pl.multiple_of(home + start, 16), n)]

    def row_gather(o, j):
        keep, send, n = rsegs[o][j]
        src = rfin.at[pl.ds(ROW_FIN[o], n)] if j == 2 else row_at(keep, n)
        return pltpu.make_async_remote_copy(
            src, row_at(keep, n), ss_r.at[o * 6 + 3 + j], rs_r.at[o * 6 + 3 + j],
            device_id=place.partner(ROW_ORDERS[o][j]), device_id_type=MESH)

    def row_local(o):
        keep, send, n = rsegs[o][2]
        return pltpu.make_async_copy(rfin.at[pl.ds(ROW_FIN[o], n)], row_at(keep, n), ls.at[RCH + CCH + o])

    def row_share(o, j):
        if j == 3:
            keep, send, n = rsegs[o][2]
            src, start = rfin.at[pl.ds(ROW_FIN[o], n)], keep
        else:
            keep, send, n = rsegs[o][j]
            src, start = row_at(send, n), send
        return pltpu.make_async_remote_copy(
            src, row_at(start, n), ss_s.at[o * 4 + j], rs_s.at[o * 4 + j], device_id=sister, device_id_type=MESH)

    def col_at(start, n):
        return colhalf.at[pl.ds(start, n)]

    def col_gather(o, j):
        keep, send, n = csegs[o][j]
        src = cfin.at[pl.ds(COL_FIN[o], n)] if j == 2 else col_at(keep, n)
        return pltpu.make_async_remote_copy(
            src, col_at(keep, n), ss_c.at[o * 6 + 3 + j], rs_c.at[o * 6 + 3 + j],
            device_id=place.partner(COL_ORDERS[o][j]), device_id_type=MESH)

    def col_local(o):
        keep, send, n = csegs[o][2]
        return pltpu.make_async_copy(cfin.at[pl.ds(COL_FIN[o], n)], col_at(keep, n), ls.at[2 * RCH + CCH + o])

    for o in range(RCH):
        row_load(o).start()
    for o in range(CCH):
        col_load(o).start()
    greet(place, ("core", "xa", "xb", "yh", "za", "zb", "yl"))
    for o in range(RCH):
        pair(o).start()
    for o in range(CCH):
        col_send(o, 0).start()
    for o in range(RCH):
        row_load(o).wait()
        pair(o).wait_recv()
        add_rows(racc, ROW_BASE[o], racc, ROW_BASE[o], rcore, ROW_BASE[o], ROW_LEN[o])
        row_send(o, 0).start()

    def col_add(o, j):
        keep, send, n = csegs[o][j]
        if j == 0:
            col_load(o).wait()
        col_send(o, j).wait_recv()
        if j < 2:
            add_rows(cacc, keep, cacc, keep, crecv, cland[o][j], n)
            col_send(o, j + 1).start()
        else:
            add_rows(cfin, COL_FIN[o], cacc, keep, crecv, cland[o][j], n)
            col_gather(o, 2).start()
            col_local(o).start()

    def row_add(o, j, total):
        keep, send, n = rsegs[o][j]
        row_send(o, j).wait_recv()
        if j < 2:
            add_rows(racc, keep, racc, keep, rrecv, rland[o][j], n)
            row_send(o, j + 1).start()
            return total

        def body(i, total):
            a = racc[pl.ds(pl.multiple_of(keep + i * 16, 16), 16), :].astype(F32)
            b = rrecv[pl.ds(pl.multiple_of(rland[o][2] + i * 16, 16), 16), :].astype(F32)
            c = a + b
            rfin[pl.ds(pl.multiple_of(ROW_FIN[o] + i * 16, 16), 16), :] = c.astype(BF16)
            c2 = c * c
            return total + c2[:8] + c2[8:]

        total = lax.fori_loop(0, n // 16, body, total)
        row_gather(o, 2).start()
        row_local(o).start()
        row_share(o, 3).start()
        return total

    total = jnp.zeros((8, SCANS), F32)
    for j in range(3):
        for o in range(max(RCH, CCH)):
            if o < CCH:
                col_add(o, j)
            if o < RCH:
                total = row_add(o, j, total)
    squares[...] = total

    def col_pass(o, j):
        if j == 2:
            col_local(o).wait()
        col_gather(o, j).wait_recv()
        if j > 0:
            col_gather(o, j - 1).start()

    def row_pass(o, j):
        if j == 2:
            row_local(o).wait()
        row_gather(o, j).wait_recv()
        if j > 0:
            row_gather(o, j - 1).start()
        row_share(o, j).start()

    for j in (2, 1, 0):
        for o in range(max(RCH, CCH)):
            if o < CCH:
                col_pass(o, j)
            if o < RCH:
                row_pass(o, j)
    for o in range(RCH):
        pair(o).wait_send()
        for j in range(4):
            row_share(o, j).wait_recv()
            row_share(o, j).wait_send()
        for j in range(3):
            row_send(o, j).wait_send()
            row_gather(o, j).wait_send()
    for o in range(CCH):
        for j in range(3):
            col_send(o, j).wait_send()
            col_gather(o, j).wait_send()


def update_kernel(rows_s, cols_s, count_s, omega_ref, rowhalf_ref, band_ref, series_ref, colhalf_ref,
                  out_ref, sums_ref, grad_ref, acc_ref, diag_ref):
    s = pl.program_id(0)
    live = s < count_s[0]
    row_base = lax.axis_index("row") * BAND
    col_base = lax.axis_index("col") * BLK

    @pl.when(s == 0)
    def _():
        acc_ref[...] = jnp.zeros_like(acc_ref)
        diag_ref[...] = jnp.zeros_like(diag_ref)

    @pl.when(jnp.logical_not(live))
    def _():
        out_ref[0] = jnp.zeros((TILE, TILE), F32)

    @pl.when(live)
    def _():
        grad_ref[...] = (0.5 / SCANS) * (
            jnp.dot(rowhalf_ref[0], series_ref[...], preferred_element_type=F32)
            + lax.dot_general(band_ref[0], colhalf_ref[0], (((0,), (0,)), ((), ())), preferred_element_type=F32)
        )
        blk = 32

        def fold(v):
            return v[0:8] + v[8:16] + v[16:24] + v[24:32]

        def body(i, carry):
            before, inner, moved, after = carry
            at = pl.ds(pl.multiple_of(i * blk, blk), blk)
            now = omega_ref[0, at, :]
            grad = grad_ref[at, :]
            stepped = now - STEP * grad
            updated = stepped - jnp.clip(stepped, -THRESH, THRESH)
            change = updated - now
            out_ref[0, at, :] = updated
            return (before + fold(jnp.abs(now)), inner + fold(grad * change), moved + fold(change * change),
                    after + fold(jnp.abs(updated)))

        zero = jnp.zeros((8, TILE), F32)
        before, inner, moved, after = lax.fori_loop(0, TILE // blk, body, (zero, zero, zero, zero))
        acc_ref[0] += before
        acc_ref[1] += inner
        acc_ref[2] += moved
        acc_ref[3] += after

        @pl.when(row_base + rows_s[s] == col_base + cols_s[s])
        def _():
            mask = lax.broadcasted_iota(jnp.int32, (128, 128), 0) == lax.broadcasted_iota(jnp.int32, (128, 128), 1)
            for q in range(TILE // 128):
                at = slice(q * 128, (q + 1) * 128)

                def pick(v):
                    return jnp.sum(jnp.where(mask, v, 0.0), axis=0, keepdims=True)

                now = pick(omega_ref[0, at, at])
                plain = pick(grad_ref[at, at])
                shrunk = out_ref[0, at, at]
                old = pick(shrunk)
                grad = plain - 1.0 / now
                stepped = now - STEP * grad
                change = stepped - now
                old_change = old - now
                out_ref[0, at, at] = jnp.where(mask, stepped, shrunk)
                diag_ref[0:1] += jnp.log(now)
                diag_ref[1:2] -= jnp.abs(now)
                diag_ref[2:3] += grad * change - plain * old_change
                diag_ref[3:4] += change * change - old_change * old_change
                diag_ref[4:5] -= jnp.abs(old)

    @pl.when(s == SLOTS - 1)
    def _():
        sums_ref[0:1] = diag_ref[0:1]
        for t in range(4):
            v = acc_ref[t]
            v = v[:, 0:128] + v[:, 128:256] + v[:, 256:384] + v[:, 384:512]
            sums_ref[1 + t:2 + t] = jnp.sum(v, axis=0, keepdims=True) + diag_ref[1 + t:2 + t]
        sums_ref[5:8] = jnp.zeros((3, 128), F32)


def total_kernel(sums, squares, out, vec, recv_a, recv_b, ss, rs):
    place = Place()
    row, col = place.row, place.col
    barrier = pltpu.get_barrier_semaphore()
    for k in range(1, 16):
        pl.semaphore_signal(barrier, inc=1, device_id=(row, (col + k) % 16), device_id_type=MESH)
    for k in range(1, 8):
        pl.semaphore_signal(barrier, inc=1, device_id=((row + k) % 8, col), device_id_type=MESH)
    v = squares[...]
    v = jnp.sum(v, axis=0, keepdims=True)
    v = v[:, 0:128] + v[:, 128:256] + v[:, 256:384]
    spot = lax.broadcasted_iota(jnp.int32, (8, 128), 0) == 5
    vec[0] = sums[...] + jnp.where(spot, jnp.broadcast_to(v, (8, 128)), 0.0)
    pl.semaphore_wait(barrier, 22)

    def across(k):
        return pltpu.make_async_remote_copy(vec.at[0], recv_a.at[col], ss.at[k - 1], rs.at[k - 1],
                                            device_id=(row, (col + k) % 16), device_id_type=MESH)

    def down(k):
        return pltpu.make_async_remote_copy(vec.at[1], recv_b.at[row], ss.at[14 + k], rs.at[14 + k],
                                            device_id=((row + k) % 8, col), device_id_type=MESH)

    for k in range(1, 16):
        across(k).start()
    recv_a[col] = vec[0]
    for k in range(1, 16):
        across(k).wait_recv()
    total = recv_a[0]
    for k in range(1, 16):
        total = total + recv_a[k]
    vec[1] = total
    for k in range(1, 8):
        down(k).start()
    recv_b[row] = total
    for k in range(1, 8):
        down(k).wait_recv()
    total = recv_b[0]
    for k in range(1, 8):
        total = total + recv_b[k]
    s = jnp.sum(total, axis=1, keepdims=True)
    smooth = -s[0:1] + s[5:6] / (2.0 * SCANS)
    objective = smooth + PENALTY * s[1:2]
    bound = smooth + s[2:3] + s[3:4] / (2.0 * STEP) + PENALTY * s[4:5]
    out[0] = objective[0, 0]
    out[1] = bound[0, 0]
    for k in range(1, 16):
        across(k).wait_send()
    for k in range(1, 8):
        down(k).wait_send()


def plain(**kw):
    return pltpu.CompilerParams(vmem_limit_bytes=60 << 20, **kw)


dma = pltpu.SemaphoreType.DMA
VMEM = pl.BlockSpec(memory_space=pltpu.VMEM)
HBM = pl.BlockSpec(memory_space=pl.ANY)


def band_call(series, cid):
    return pl.pallas_call(
        band_kernel,
        out_shape=jax.ShapeDtypeStruct((BAND, SCANS, TILE), BF16),
        in_specs=[HBM], out_specs=HBM,
        scratch_shapes=[pltpu.VMEM((SCANS, BLK * TILE), BF16),
                        dma((CHUNKS,)), dma((CHUNKS,)), dma((CHUNKS,)), dma((CHUNKS,)), dma((CHUNKS,)),
                        dma((CHUNKS + 1,))],
        compiler_params=plain(collective_id=cid, has_side_effects=True), name="band",
    )(series)


def sums_call(row_part, col_part, cid):
    return pl.pallas_call(
        sums_kernel,
        out_shape=(jax.ShapeDtypeStruct((ROWS, SCANS), BF16), jax.ShapeDtypeStruct((COLS, TILE), BF16),
                   jax.ShapeDtypeStruct((8, SCANS), F32)),
        in_specs=[HBM, HBM], out_specs=(HBM, HBM, VMEM),
        scratch_shapes=[pltpu.VMEM((HALF, SCANS), BF16), pltpu.VMEM((HALF, SCANS), BF16),
                        pltpu.VMEM((HALF * 7 // 8, SCANS), BF16), pltpu.VMEM((HALF // 8, SCANS), BF16),
                        pltpu.VMEM((COLS, TILE), BF16), pltpu.VMEM((COLS * 7 // 8, TILE), BF16),
                        pltpu.VMEM((COLS // 8, TILE), BF16),
                        dma((RCH,)), dma((RCH,)), dma((6 * RCH,)), dma((6 * RCH,)),
                        dma((4 * RCH,)), dma((4 * RCH,)), dma((6 * CCH,)), dma((6 * CCH,)),
                        dma((2 * RCH + 2 * CCH,))],
        compiler_params=plain(collective_id=cid, has_side_effects=True), name="sums",
    )(row_part, col_part)


def local(series, omega_tiles, tile_row, tile_col, tile_count):
    omega = omega_tiles[0, 0]
    rows_s = tile_row[0, 0]
    cols_s = tile_col[0, 0]
    count = tile_count[0]
    band = band_call(series, 0)
    row_part, col_part = pl.pallas_call(
        partial_kernel,
        out_shape=(jax.ShapeDtypeStruct((BAND, TILE, SCANS), BF16), jax.ShapeDtypeStruct((BLK, SCANS, TILE), BF16)),
        grid_spec=pltpu.PrefetchScalarGridSpec(
            num_scalar_prefetch=3, grid=(SLOTS,),
            in_specs=[pl.BlockSpec((1, TILE, TILE), lambda s, *_: (s, 0, 0)),
                      pl.BlockSpec((SCANS, BLK * TILE), lambda s, *_: (0, 0)),
                      pl.BlockSpec((1, SCANS, TILE), lambda s, r, c, m: (r[s], 0, 0))],
            out_specs=(pl.BlockSpec((BAND, TILE, SCANS), lambda s, *_: (0, 0, 0)),
                       pl.BlockSpec((BLK, SCANS, TILE), lambda s, *_: (0, 0, 0))),
            scratch_shapes=[pltpu.VMEM((BAND, TILE, SCANS), F32), pltpu.VMEM((BLK, SCANS, TILE), F32)]),
        compiler_params=plain(), name="partials",
    )(rows_s, cols_s, count, omega, series, band)

    row_half, col_half, squares = sums_call(row_part.reshape(ROWS, SCANS), col_part.reshape(COLS, TILE), 1)
    omega_next, sums = pl.pallas_call(
        update_kernel,
        out_shape=(jax.ShapeDtypeStruct((SLOTS, TILE, TILE), F32), jax.ShapeDtypeStruct((8, 128), F32)),
        grid_spec=pltpu.PrefetchScalarGridSpec(
            num_scalar_prefetch=3, grid=(SLOTS,),
            in_specs=[pl.BlockSpec((1, TILE, TILE), lambda s, *_: (s, 0, 0)),
                      pl.BlockSpec((1, TILE, SCANS), lambda s, r, c, m: (r[s], 0, 0)),
                      pl.BlockSpec((1, SCANS, TILE), lambda s, r, c, m: (r[s], 0, 0)),
                      pl.BlockSpec((SCANS, TILE), lambda s, r, c, m: (0, c[s])),
                      pl.BlockSpec((1, SCANS, TILE), lambda s, r, c, m: (c[s], 0, 0))],
            out_specs=(pl.BlockSpec((1, TILE, TILE), lambda s, *_: (s, 0, 0)),
                       pl.BlockSpec((8, 128), lambda s, *_: (0, 0))),
            scratch_shapes=[pltpu.VMEM((TILE, TILE), F32), pltpu.VMEM((4, 8, TILE), F32), pltpu.VMEM((8, 128), F32)]),
        compiler_params=plain(), name="update",
    )(rows_s, cols_s, count, omega, row_half.reshape(BAND, TILE, SCANS), band, series, col_half.reshape(BLK, SCANS, TILE))

    values = pl.pallas_call(
        total_kernel,
        out_shape=jax.ShapeDtypeStruct((2,), F32),
        in_specs=[VMEM, VMEM], out_specs=pl.BlockSpec(memory_space=pltpu.SMEM),
        scratch_shapes=[pltpu.VMEM((2, 8, 128), F32), pltpu.VMEM((16, 8, 128), F32), pltpu.VMEM((8, 8, 128), F32),
                        pltpu.SemaphoreType.DMA((22,)), pltpu.SemaphoreType.DMA((22,))],
        compiler_params=plain(collective_id=2, has_side_effects=True), name="total",
    )(sums, squares)
    return omega_next[None, None], values


def solution(mesh):
    placed = (
        P(None, "col"),
        P("row", "col", None, None, None),
        P("row", "col", None),
        P("row", "col", None),
        P("row", "col"),
    )
    return jax.shard_map(
        local,
        mesh=mesh,
        in_specs=placed,
        out_specs=(P("row", "col", None, None, None), P()),
        check_vma=False,
    )
```

```python
import functools

import jax
import jax.numpy as jnp
from jax import lax
from jax.experimental import pallas as pl
from jax.experimental.pallas import tpu as pltpu
from jax.sharding import PartitionSpec as P

MESH = pl.DeviceIdType.MESH
F32 = jnp.float32
BF16 = jnp.bfloat16

STEP = 0.1
PENALTY = 0.3
THRESH = STEP * PENALTY

TILE = 512
BLK = 7
BAND = 14
SLOTS = 10
SCANS = 384

ROWS = BAND * TILE
HALF = ROWS // 2
ROW_LEN = (1152, 1152, 1280)
COLS = BLK * SCANS
COL_LEN = (512, 512, 384, 512, 384, 384)
SPLIT = 4
CHUNKS = BLK * SPLIT
CH = SCANS // SPLIT


def bases(lengths):
    out, at = [], 0
    for n in lengths:
        out.append(at)
        at += n
    return out


ROW_BASE = bases(ROW_LEN)
COL_BASE = bases(COL_LEN)
ROW_FIN = bases([n // 8 for n in ROW_LEN])
COL_FIN = bases([n // 8 for n in COL_LEN])
RCH = len(ROW_LEN)
CCH = len(COL_LEN)


class Place:
    def __init__(self):
        self.row = lax.axis_index("row")
        self.col = lax.axis_index("col")
        self.yl = self.row // 4
        self.z = self.row % 4
        self.x = self.col // 4
        self.yh = (self.col // 2) % 2
        self.core = self.col % 2
        self.bits = {
            "xa": ((self.x + 1) // 2) % 2,
            "xb": self.x // 2,
            "yh": self.yh,
            "za": ((self.z + 1) // 2) % 2,
            "zb": self.z // 2,
            "yl": self.yl,
            "core": self.core,
        }

    def at(self, x=None, yh=None, core=None, yl=None, z=None):
        x = self.x if x is None else x
        yh = self.yh if yh is None else yh
        core = self.core if core is None else core
        yl = self.yl if yl is None else yl
        z = self.z if z is None else z
        return (yl * 4 + z, x * 4 + yh * 2 + core)

    def partner(self, dim):
        if dim == "core":
            return self.at(core=1 - self.core)
        if dim == "yh":
            return self.at(yh=1 - self.yh)
        if dim == "yl":
            return self.at(yl=1 - self.yl)
        if dim == "xa":
            return self.at(x=self.x + 1 - 2 * (self.x % 2))
        if dim == "xb":
            return self.at(x=(self.x + 3 + 2 * (self.x % 2)) % 4)
        if dim == "za":
            return self.at(z=self.z + 1 - 2 * (self.z % 2))
        return self.at(z=(self.z + 3 + 2 * (self.z % 2)) % 4)


ROW_ORDERS = (("xa", "xb", "yh"), ("xb", "yh", "xa"), ("yh", "xa", "xb"))
COL_ORDERS = (("za", "zb", "yl"), ("zb", "za", "yl")) * 3


def greet(place, dims):
    barrier = pltpu.get_barrier_semaphore()
    for dim in dims:
        pl.semaphore_signal(barrier, inc=1, device_id=place.partner(dim), device_id_type=MESH)
    pl.semaphore_wait(barrier, len(dims))


def segments(place, base, length, dims):
    out = []
    start, n = base, length
    for dim in dims:
        n = n // 2
        bit = place.bits[dim]
        keep = pl.multiple_of(start + bit * n, 16)
        send = pl.multiple_of(start + (1 - bit) * n, 16)
        out.append((keep, send, n))
        start = keep
    return out


def block_of(n):
    for blk in (128, 112, 96, 80, 64, 48, 32, 16):
        if n % blk == 0:
            return blk
    return n


def add_rows(dst, dst_at, one, one_at, two, two_at, n):
    blk = block_of(n)

    def body(i, carry):
        o = i * blk
        a = one[pl.ds(pl.multiple_of(one_at + o, 16), blk), :].astype(F32)
        b = two[pl.ds(pl.multiple_of(two_at + o, 16), blk), :].astype(F32)
        dst[pl.ds(pl.multiple_of(dst_at + o, 16), blk), :] = (a + b).astype(dst.dtype)
        return carry

    lax.fori_loop(0, n // blk, body, 0)


def partial_kernel(rows_s, cols_s, count_s, omega_h, series_h, band_h, row_ref, col_ref, omega_ref, series_ref, band_ref,
                   racc_ref, cacc_ref, rout_ref, cout_ref, isem, rsem, csem):
    count = count_s[0]

    def loads(s):
        at = pl.multiple_of(cols_s[s] * TILE, TILE)
        return (pltpu.make_async_copy(omega_h.at[s], omega_ref.at[s], isem.at[s, 0]),
                pltpu.make_async_copy(series_h.at[:, pl.ds(at, TILE)], series_ref.at[s], isem.at[s, 1]),
                pltpu.make_async_copy(band_h.at[rows_s[s]], band_ref.at[s], isem.at[s, 2]))

    def fetch(s, carry):
        for load in loads(s):
            load.start()
        return carry

    lax.fori_loop(0, count, fetch, 0)

    def row_out(i):
        return pltpu.make_async_copy(rout_ref.at[i], row_ref.at[i], rsem.at[i])

    def col_out(i):
        return pltpu.make_async_copy(cout_ref.at[i], col_ref.at[i], csem.at[i])

    def clear(ids, stage, out, blocks):
        def one(i, carry):
            held = False
            for k in range(SLOTS):
                held = jnp.logical_or(held, jnp.logical_and(k < count, ids[k] == i))

            @pl.when(jnp.logical_not(held))
            def _():
                stage[i] = jnp.zeros(stage.shape[1:], BF16)
                out(i).start()

            return carry

        lax.fori_loop(0, blocks, one, 0)

    clear(rows_s, rout_ref, row_out, BAND)
    clear(cols_s, cout_ref, col_out, BLK)

    def again(ids, t):
        seen, more = False, False
        for k in range(SLOTS):
            same = ids[k] == ids[t]
            seen = jnp.logical_or(seen, jnp.logical_and(k < t, same))
            more = jnp.logical_or(more, jnp.logical_and(jnp.logical_and(k > t, k < count), same))
        return seen, jnp.logical_not(more)

    def work(s, carry):
        for load in loads(s):
            load.wait()
        half = omega_ref[s].astype(BF16)
        panel = series_ref[s]
        row_again, row_last = again(rows_s, s)
        col_again, col_last = again(cols_s, s)
        term = lax.dot_general(half, panel, (((1,), (1,)), ((), ())), preferred_element_type=F32)

        @pl.when(row_again)
        def _():
            racc_ref[rows_s[s]] += term

        @pl.when(jnp.logical_not(row_again))
        def _():
            racc_ref[rows_s[s]] = term

        term2 = jnp.dot(band_ref[s], half, preferred_element_type=F32)

        @pl.when(col_again)
        def _():
            cacc_ref[cols_s[s]] += term2

        @pl.when(jnp.logical_not(col_again))
        def _():
            cacc_ref[cols_s[s]] = term2

        @pl.when(row_last)
        def _():
            rout_ref[rows_s[s]] = racc_ref[rows_s[s]].astype(BF16)
            row_out(rows_s[s]).start()

        @pl.when(col_last)
        def _():
            cout_ref[cols_s[s]] = cacc_ref[cols_s[s]].astype(BF16)
            col_out(cols_s[s]).start()

        return carry

    lax.fori_loop(0, count, work, 0)
    for i in range(BAND):
        row_out(i).wait()
    for i in range(BLK):
        col_out(i).wait()


def band_kernel(series, band, sbuf, ss_b, rs_b, ss_y, ss_s, rs_s, ls):
    place = Place()
    core = place.core
    xs = place.yl * 2 + place.z // 2
    near = place.yh == place.z % 2
    source = jnp.logical_and(place.x == xs, near)
    sister = place.partner("core")
    over = place.partner("yh")
    dist = [(place.x - xs + 4) % 4, (xs - place.x + 4) % 4]
    onward = [place.at(x=(place.x + 1) % 4), place.at(x=(place.x + 3) % 4)]
    hops = [jnp.where(near, dist[s % 2], (dist[s % 2] + 4 - s // 2) % 4) for s in range(4)]
    lag = [jnp.where(near, 0, s // 2 + 1) + hops[s] for s in range(4)]
    crossing = [jnp.logical_and(near, dist[s % 2] == s // 2) for s in range(4)]

    def slot(i, which):
        return band.at[which * BLK + i // SPLIT, pl.ds(pl.multiple_of((i % SPLIT) * CH, 16), CH), :]

    def native(i, held):
        return held.at[pl.ds(pl.multiple_of((i % SPLIT) * CH, 16), CH),
                       pl.ds(pl.multiple_of((i // SPLIT) * TILE, TILE), TILE)]

    def to_next(src, i, s):
        return pltpu.make_async_remote_copy(src, slot(i, core), ss_b.at[i], rs_b.at[i],
                                            device_id=onward[s % 2], device_id_type=MESH)

    def to_over(src, i):
        return pltpu.make_async_remote_copy(src, slot(i, core), ss_y.at[i], rs_b.at[i],
                                            device_id=over, device_id_type=MESH)

    def to_sister(src, i):
        return pltpu.make_async_remote_copy(src, slot(i, core), ss_s.at[i], rs_s.at[i],
                                            device_id=sister, device_id_type=MESH)

    def keep_native(i):
        return pltpu.make_async_copy(native(i, sbuf), slot(i, core), ls.at[1 + i])

    load = pltpu.make_async_copy(series, sbuf, ls.at[0])

    @pl.when(source)
    def _():
        load.start()

    greet(place, ("core", "xa", "xb", "yh"))

    def forward(src, i, s):
        @pl.when(hops[s] < 3)
        def _():
            to_next(src, i, s).start()

        @pl.when(crossing[s])
        def _():
            to_over(src, i).start()

        to_sister(src, i).start()

    @pl.when(source)
    def _():
        def emit(k, carry):
            for s in range(4):
                i = k * 4 + s
                forward(native(i, series), i, s)
            return carry

        lax.fori_loop(0, CHUNKS // 4, emit, 0)
        load.wait()

        def hold(i, carry):
            keep_native(i).start()
            return carry

        lax.fori_loop(0, CHUNKS, hold, 0)

    @pl.when(jnp.logical_not(source))
    def _():
        def tick(t, carry):
            for s in range(4):
                k = t - lag[s]

                @pl.when(jnp.logical_and(k >= 0, k < CHUNKS // 4))
                def _():
                    i = k * 4 + s
                    to_next(slot(i, core), i, s).wait_recv()
                    forward(slot(i, core), i, s)

            return carry

        lax.fori_loop(0, CHUNKS // 4 + 5, tick, 0)

    def drain(k, carry):
        for s in range(4):
            i = k * 4 + s
            to_sister(slot(i, 1 - core), i).wait_recv()
            to_sister(slot(i, core), i).wait_send()

            @pl.when(hops[s] < 3)
            def _():
                to_next(slot(i, core), i, s).wait_send()

            @pl.when(crossing[s])
            def _():
                to_over(slot(i, core), i).wait_send()

            @pl.when(source)
            def _():
                keep_native(i).wait()

        return carry

    lax.fori_loop(0, CHUNKS // 4, drain, 0)


def sums_kernel(rowpart, colpart, rowhalf, colhalf, squares, racc, rcore, rrecv, rfin, cacc, crecv, cfin,
                ss_k, rs_k, ss_r, rs_r, ss_s, rs_s, ss_c, rs_c, ls):
    place = Place()
    core = place.core
    sister = place.partner("core")
    home = core * HALF
    away = (1 - core) * HALF

    rsegs = [segments(place, ROW_BASE[o], ROW_LEN[o], ROW_ORDERS[o]) for o in range(RCH)]
    csegs = [segments(place, COL_BASE[o], COL_LEN[o], COL_ORDERS[o]) for o in range(CCH)]

    def landing(segs):
        out, at = [], 0
        for line in segs:
            row = []
            for keep, send, n in line:
                row.append(at)
                at += n
            out.append(row)
        return out

    rland = landing(rsegs)
    cland = landing(csegs)

    def part_at(which, o):
        return rowpart.at[pl.ds(pl.multiple_of(which + ROW_BASE[o], 16), ROW_LEN[o])]

    def pair(o):
        at = pl.ds(ROW_BASE[o], ROW_LEN[o])
        return pltpu.make_async_remote_copy(part_at(away, o), rcore.at[at], ss_k.at[o], rs_k.at[o],
                                            device_id=sister, device_id_type=MESH)

    def row_load(o):
        at = pl.ds(ROW_BASE[o], ROW_LEN[o])
        return pltpu.make_async_copy(part_at(home, o), racc.at[at], ls.at[o])

    def col_load(o):
        keep, send, n = csegs[o][0]
        return pltpu.make_async_copy(colpart.at[pl.ds(keep, n)], cacc.at[pl.ds(keep, n)], ls.at[RCH + o])

    def row_send(o, j):
        keep, send, n = rsegs[o][j]
        return pltpu.make_async_remote_copy(
            racc.at[pl.ds(send, n)], rrecv.at[pl.ds(rland[o][j], n)], ss_r.at[o * 6 + j], rs_r.at[o * 6 + j],
            device_id=place.partner(ROW_ORDERS[o][j]), device_id_type=MESH)

    def col_send(o, j):
        keep, send, n = csegs[o][j]
        src = colpart if j == 0 else cacc
        return pltpu.make_async_remote_copy(
            src.at[pl.ds(send, n)], crecv.at[pl.ds(cland[o][j], n)], ss_c.at[o * 6 + j], rs_c.at[o * 6 + j],
            device_id=place.partner(COL_ORDERS[o][j]), device_id_type=MESH)

    def row_at(start, n):
        return rowhalf.at[pl.ds(pl.multiple_of(home + start, 16), n)]

    def row_gather(o, j):
        keep, send, n = rsegs[o][j]
        src = rfin.at[pl.ds(ROW_FIN[o], n)] if j == 2 else row_at(keep, n)
        return pltpu.make_async_remote_copy(
            src, row_at(keep, n), ss_r.at[o * 6 + 3 + j], rs_r.at[o * 6 + 3 + j],
            device_id=place.partner(ROW_ORDERS[o][j]), device_id_type=MESH)

    def row_local(o):
        keep, send, n = rsegs[o][2]
        return pltpu.make_async_copy(rfin.at[pl.ds(ROW_FIN[o], n)], row_at(keep, n), ls.at[RCH + CCH + o])

    def row_share(o, j):
        if j == 3:
            keep, send, n = rsegs[o][2]
            src, start = rfin.at[pl.ds(ROW_FIN[o], n)], keep
        else:
            keep, send, n = rsegs[o][j]
            src, start = row_at(send, n), send
        return pltpu.make_async_remote_copy(
            src, row_at(start, n), ss_s.at[o * 4 + j], rs_s.at[o * 4 + j], device_id=sister, device_id_type=MESH)

    def col_at(start, n):
        return colhalf.at[pl.ds(start, n)]

    def col_gather(o, j):
        keep, send, n = csegs[o][j]
        src = cfin.at[pl.ds(COL_FIN[o], n)] if j == 2 else col_at(keep, n)
        return pltpu.make_async_remote_copy(
            src, col_at(keep, n), ss_c.at[o * 6 + 3 + j], rs_c.at[o * 6 + 3 + j],
            device_id=place.partner(COL_ORDERS[o][j]), device_id_type=MESH)

    def col_local(o):
        keep, send, n = csegs[o][2]
        return pltpu.make_async_copy(cfin.at[pl.ds(COL_FIN[o], n)], col_at(keep, n), ls.at[2 * RCH + CCH + o])

    for o in range(RCH):
        row_load(o).start()
    for o in range(CCH):
        col_load(o).start()
    greet(place, ("core", "xa", "xb", "yh", "za", "zb", "yl"))
    for o in range(RCH):
        pair(o).start()
    for o in range(CCH):
        col_send(o, 0).start()
    for o in range(RCH):
        row_load(o).wait()
        pair(o).wait_recv()
        add_rows(racc, ROW_BASE[o], racc, ROW_BASE[o], rcore, ROW_BASE[o], ROW_LEN[o])
        row_send(o, 0).start()

    def col_add(o, j):
        keep, send, n = csegs[o][j]
        if j == 0:
            col_load(o).wait()
        col_send(o, j).wait_recv()
        if j < 2:
            add_rows(cacc, keep, cacc, keep, crecv, cland[o][j], n)
            col_send(o, j + 1).start()
        else:
            add_rows(cfin, COL_FIN[o], cacc, keep, crecv, cland[o][j], n)
            col_gather(o, 2).start()
            col_local(o).start()

    def row_add(o, j, total):
        keep, send, n = rsegs[o][j]
        row_send(o, j).wait_recv()
        if j < 2:
            add_rows(racc, keep, racc, keep, rrecv, rland[o][j], n)
            row_send(o, j + 1).start()
            return total

        def body(i, total):
            a = racc[pl.ds(pl.multiple_of(keep + i * 16, 16), 16), :].astype(F32)
            b = rrecv[pl.ds(pl.multiple_of(rland[o][2] + i * 16, 16), 16), :].astype(F32)
            c = a + b
            rfin[pl.ds(pl.multiple_of(ROW_FIN[o] + i * 16, 16), 16), :] = c.astype(BF16)
            c2 = c * c
            return total + c2[:8] + c2[8:]

        total = lax.fori_loop(0, n // 16, body, total)
        row_gather(o, 2).start()
        row_local(o).start()
        row_share(o, 3).start()
        return total

    total = jnp.zeros((8, SCANS), F32)
    for j in range(3):
        for o in range(max(RCH, CCH)):
            if o < CCH:
                col_add(o, j)
            if o < RCH:
                total = row_add(o, j, total)
    squares[...] = total

    def col_pass(o, j):
        if j == 2:
            col_local(o).wait()
        col_gather(o, j).wait_recv()
        if j > 0:
            col_gather(o, j - 1).start()

    def row_pass(o, j):
        if j == 2:
            row_local(o).wait()
        row_gather(o, j).wait_recv()
        if j > 0:
            row_gather(o, j - 1).start()
        row_share(o, j).start()

    for j in (2, 1, 0):
        for o in range(max(RCH, CCH)):
            if o < CCH:
                col_pass(o, j)
            if o < RCH:
                row_pass(o, j)
    for o in range(RCH):
        pair(o).wait_send()
        for j in range(4):
            row_share(o, j).wait_recv()
            row_share(o, j).wait_send()
        for j in range(3):
            row_send(o, j).wait_send()
            row_gather(o, j).wait_send()
    for o in range(CCH):
        for j in range(3):
            col_send(o, j).wait_send()
            col_gather(o, j).wait_send()


def update_kernel(rows_s, cols_s, count_s, omega_h, rowhalf_h, band_h, series_h, colhalf_h, out_h, sums_ref,
                  omega_ref, rowhalf_ref, band_ref, series_ref, colhalf_ref, out_ref, zero_ref,
                  grad_ref, acc_ref, diag_ref, isem, osem):
    count = count_s[0]
    row_base = lax.axis_index("row") * BAND
    col_base = lax.axis_index("col") * BLK

    def loads(s):
        at = pl.multiple_of(cols_s[s] * TILE, TILE)
        return (pltpu.make_async_copy(omega_h.at[s], omega_ref.at[s], isem.at[s, 0]),
                pltpu.make_async_copy(rowhalf_h.at[rows_s[s]], rowhalf_ref.at[s], isem.at[s, 1]),
                pltpu.make_async_copy(band_h.at[rows_s[s]], band_ref.at[s], isem.at[s, 2]),
                pltpu.make_async_copy(series_h.at[:, pl.ds(at, TILE)], series_ref.at[s], isem.at[s, 3]),
                pltpu.make_async_copy(colhalf_h.at[cols_s[s]], colhalf_ref.at[s], isem.at[s, 4]))

    def store(s):
        return pltpu.make_async_copy(out_ref.at[s], out_h.at[s], osem.at[s])

    def store_zero(s):
        return pltpu.make_async_copy(zero_ref, out_h.at[s], osem.at[s])

    def fetch(s, carry):
        for load in loads(s):
            load.start()
        return carry

    lax.fori_loop(0, count, fetch, 0)
    zero_ref[...] = jnp.zeros_like(zero_ref)
    acc_ref[...] = jnp.zeros_like(acc_ref)
    diag_ref[...] = jnp.zeros_like(diag_ref)

    def clear(s, carry):
        store_zero(s).start()
        return carry

    lax.fori_loop(count, SLOTS, clear, 0)

    def work(s, carry):
        for load in loads(s):
            load.wait()
        panel = series_ref[s]
        sums = colhalf_ref[s]
        blk = 128

        def fold(v):
            return jnp.sum(v.reshape(blk // 8, 8, TILE), axis=0)

        before, model, after = acc_ref[0], acc_ref[1], acc_ref[2]
        for i in range(TILE // blk):
            at = slice(i * blk, (i + 1) * blk)
            grad = (0.5 / SCANS) * (
                jnp.dot(rowhalf_ref[s, at, :], panel, preferred_element_type=F32)
                + lax.dot_general(band_ref[s, :, at], sums, (((0,), (0,)), ((), ())), preferred_element_type=F32)
            )
            now = omega_ref[s, at, :]
            grad_ref[at, :] = grad
            stepped = now - STEP * grad
            updated = stepped - jnp.clip(stepped, -THRESH, THRESH)
            change = updated - now
            out_ref[s, at, :] = updated
            before += fold(jnp.abs(now))
            model += fold(change * (grad + change * (0.5 / STEP)))
            after += fold(jnp.abs(updated))
        acc_ref[0] = before
        acc_ref[1] = model
        acc_ref[2] = after

        @pl.when(row_base + rows_s[s] == col_base + cols_s[s])
        def _():
            mask = lax.broadcasted_iota(jnp.int32, (128, 128), 0) == lax.broadcasted_iota(jnp.int32, (128, 128), 1)
            for q in range(TILE // 128):
                at = slice(q * 128, (q + 1) * 128)

                def pick(v):
                    return jnp.sum(jnp.where(mask, v, 0.0), axis=0, keepdims=True)

                now = pick(omega_ref[s, at, at])
                plain = pick(grad_ref[at, at])
                shrunk = out_ref[s, at, at]
                old = pick(shrunk)
                grad = plain - 1.0 / now
                stepped = now - STEP * grad
                change = stepped - now
                old_change = old - now
                out_ref[s, at, at] = jnp.where(mask, stepped, shrunk)
                diag_ref[0:1] += jnp.log(now)
                diag_ref[1:2] -= jnp.abs(now)
                diag_ref[2:3] += (change * (grad + change * (0.5 / STEP))
                                  - old_change * (plain + old_change * (0.5 / STEP)))
                diag_ref[3:4] -= jnp.abs(old)

        store(s).start()
        return carry

    lax.fori_loop(0, count, work, 0)
    sums_ref[0:1] = diag_ref[0:1]
    for t in range(3):
        v = acc_ref[t]
        v = v[:, 0:128] + v[:, 128:256] + v[:, 256:384] + v[:, 384:512]
        sums_ref[1 + t:2 + t] = jnp.sum(v, axis=0, keepdims=True) + diag_ref[1 + t:2 + t]
    sums_ref[4:8] = jnp.zeros((4, 128), F32)

    def done(s, carry):
        store(s).wait()
        return carry

    def cleared(s, carry):
        store_zero(s).wait()
        return carry

    lax.fori_loop(0, count, done, 0)
    lax.fori_loop(count, SLOTS, cleared, 0)


def total_kernel(sums, squares, out, vec, recv_a, recv_b, ss, rs):
    place = Place()
    row, col = place.row, place.col
    barrier = pltpu.get_barrier_semaphore()
    for k in range(1, 16):
        pl.semaphore_signal(barrier, inc=1, device_id=(row, (col + k) % 16), device_id_type=MESH)
    for k in range(1, 8):
        pl.semaphore_signal(barrier, inc=1, device_id=((row + k) % 8, col), device_id_type=MESH)
    v = squares[...]
    v = jnp.sum(v, axis=0, keepdims=True)
    v = v[:, 0:128] + v[:, 128:256] + v[:, 256:384]
    spot = lax.broadcasted_iota(jnp.int32, (8, 128), 0) == 5
    vec[0] = sums[...] + jnp.where(spot, jnp.broadcast_to(v, (8, 128)), 0.0)
    pl.semaphore_wait(barrier, 22)

    def across(k):
        return pltpu.make_async_remote_copy(vec.at[0], recv_a.at[col], ss.at[k - 1], rs.at[k - 1],
                                            device_id=(row, (col + k) % 16), device_id_type=MESH)

    def down(k):
        return pltpu.make_async_remote_copy(vec.at[1], recv_b.at[row], ss.at[14 + k], rs.at[14 + k],
                                            device_id=((row + k) % 8, col), device_id_type=MESH)

    for k in range(1, 16):
        across(k).start()
    recv_a[col] = vec[0]
    for k in range(1, 16):
        across(k).wait_recv()
    total = recv_a[0]
    for k in range(1, 16):
        total = total + recv_a[k]
    vec[1] = total
    for k in range(1, 8):
        down(k).start()
    recv_b[row] = total
    for k in range(1, 8):
        down(k).wait_recv()
    total = recv_b[0]
    for k in range(1, 8):
        total = total + recv_b[k]
    s = jnp.sum(total, axis=1, keepdims=True)
    smooth = -s[0:1] + s[5:6] / (2.0 * SCANS)
    objective = smooth + PENALTY * s[1:2]
    bound = smooth + s[2:3] + PENALTY * s[3:4]
    out[0] = objective[0, 0]
    out[1] = bound[0, 0]
    for k in range(1, 16):
        across(k).wait_send()
    for k in range(1, 8):
        down(k).wait_send()


def plain(**kw):
    return pltpu.CompilerParams(vmem_limit_bytes=60 << 20, **kw)


dma = pltpu.SemaphoreType.DMA
VMEM = pl.BlockSpec(memory_space=pltpu.VMEM)
HBM = pl.BlockSpec(memory_space=pl.ANY)


def band_call(series, cid):
    return pl.pallas_call(
        band_kernel,
        out_shape=jax.ShapeDtypeStruct((BAND, SCANS, TILE), BF16),
        in_specs=[HBM], out_specs=HBM,
        scratch_shapes=[pltpu.VMEM((SCANS, BLK * TILE), BF16),
                        dma((CHUNKS,)), dma((CHUNKS,)), dma((CHUNKS,)), dma((CHUNKS,)), dma((CHUNKS,)),
                        dma((CHUNKS + 1,))],
        compiler_params=plain(collective_id=cid, has_side_effects=True), name="band",
    )(series)


def sums_call(row_part, col_part, cid):
    return pl.pallas_call(
        sums_kernel,
        out_shape=(jax.ShapeDtypeStruct((ROWS, SCANS), BF16), jax.ShapeDtypeStruct((COLS, TILE), BF16),
                   jax.ShapeDtypeStruct((8, SCANS), F32)),
        in_specs=[HBM, HBM], out_specs=(HBM, HBM, VMEM),
        scratch_shapes=[pltpu.VMEM((HALF, SCANS), BF16), pltpu.VMEM((HALF, SCANS), BF16),
                        pltpu.VMEM((HALF * 7 // 8, SCANS), BF16), pltpu.VMEM((HALF // 8, SCANS), BF16),
                        pltpu.VMEM((COLS, TILE), BF16), pltpu.VMEM((COLS * 7 // 8, TILE), BF16),
                        pltpu.VMEM((COLS // 8, TILE), BF16),
                        dma((RCH,)), dma((RCH,)), dma((6 * RCH,)), dma((6 * RCH,)),
                        dma((4 * RCH,)), dma((4 * RCH,)), dma((6 * CCH,)), dma((6 * CCH,)),
                        dma((2 * RCH + 2 * CCH,))],
        compiler_params=plain(collective_id=cid, has_side_effects=True), name="sums",
    )(row_part, col_part)


def partials_call(rows_s, cols_s, count, omega, series, band):
    return pl.pallas_call(
        partial_kernel,
        out_shape=(jax.ShapeDtypeStruct((BAND, TILE, SCANS), BF16), jax.ShapeDtypeStruct((BLK, SCANS, TILE), BF16)),
        grid_spec=pltpu.PrefetchScalarGridSpec(
            num_scalar_prefetch=3, grid=(),
            in_specs=[HBM, HBM, HBM],
            out_specs=(HBM, HBM),
            scratch_shapes=[pltpu.VMEM((SLOTS, TILE, TILE), F32), pltpu.VMEM((SLOTS, SCANS, TILE), BF16),
                            pltpu.VMEM((SLOTS, SCANS, TILE), BF16),
                            pltpu.VMEM((BAND, TILE, SCANS), F32), pltpu.VMEM((BLK, SCANS, TILE), F32),
                            pltpu.VMEM((BAND, TILE, SCANS), BF16), pltpu.VMEM((BLK, SCANS, TILE), BF16),
                            dma((SLOTS, 3)), dma((BAND,)), dma((BLK,))]),
        compiler_params=plain(), name="partials",
    )(rows_s, cols_s, count, omega, series, band)


def update_call(rows_s, cols_s, count, omega, row_half, band, series, col_half):
    return pl.pallas_call(
        update_kernel,
        out_shape=(jax.ShapeDtypeStruct((SLOTS, TILE, TILE), F32), jax.ShapeDtypeStruct((8, 128), F32)),
        grid_spec=pltpu.PrefetchScalarGridSpec(
            num_scalar_prefetch=3, grid=(),
            in_specs=[HBM, HBM, HBM, HBM, HBM],
            out_specs=(HBM, VMEM),
            scratch_shapes=[pltpu.VMEM((SLOTS, TILE, TILE), F32), pltpu.VMEM((SLOTS, TILE, SCANS), BF16),
                            pltpu.VMEM((SLOTS, SCANS, TILE), BF16), pltpu.VMEM((SLOTS, SCANS, TILE), BF16),
                            pltpu.VMEM((SLOTS, SCANS, TILE), BF16), pltpu.VMEM((SLOTS, TILE, TILE), F32),
                            pltpu.VMEM((TILE, TILE), F32),
                            pltpu.VMEM((TILE, TILE), F32), pltpu.VMEM((3, 8, TILE), F32), pltpu.VMEM((8, 128), F32),
                            dma((SLOTS, 5)), dma((SLOTS,))]),
        compiler_params=plain(), name="update",
    )(rows_s, cols_s, count, omega, row_half.reshape(BAND, TILE, SCANS), band, series, col_half.reshape(BLK, SCANS, TILE))


def local(series, omega_tiles, tile_row, tile_col, tile_count):
    omega = omega_tiles[0, 0]
    rows_s = tile_row[0, 0]
    cols_s = tile_col[0, 0]
    count = tile_count[0]
    band = band_call(series, 0)
    row_part, col_part = partials_call(rows_s, cols_s, count, omega, series, band)
    row_half, col_half, squares = sums_call(row_part.reshape(ROWS, SCANS), col_part.reshape(COLS, TILE), 1)
    omega_next, sums = update_call(rows_s, cols_s, count, omega, row_half, band, series, col_half)
    values = pl.pallas_call(
        total_kernel,
        out_shape=jax.ShapeDtypeStruct((2,), F32),
        in_specs=[VMEM, VMEM], out_specs=pl.BlockSpec(memory_space=pltpu.SMEM),
        scratch_shapes=[pltpu.VMEM((2, 8, 128), F32), pltpu.VMEM((16, 8, 128), F32), pltpu.VMEM((8, 8, 128), F32),
                        pltpu.SemaphoreType.DMA((22,)), pltpu.SemaphoreType.DMA((22,))],
        compiler_params=plain(collective_id=2, has_side_effects=True), name="total",
    )(sums, squares)
    return omega_next[None, None], values


def solution(mesh):
    placed = (
        P(None, "col"),
        P("row", "col", None, None, None),
        P("row", "col", None),
        P("row", "col", None),
        P("row", "col"),
    )
    return jax.shard_map(
        local,
        mesh=mesh,
        in_specs=placed,
        out_specs=(P("row", "col", None, None, None), P()),
        check_vma=False,
    )
```

```python
import functools

import jax
import jax.numpy as jnp
from jax import lax
from jax.experimental import pallas as pl
from jax.experimental.pallas import tpu as pltpu
from jax.sharding import PartitionSpec as P

MESH = pl.DeviceIdType.MESH
F32 = jnp.float32
BF16 = jnp.bfloat16

STEP = 0.1
PENALTY = 0.3
THRESH = STEP * PENALTY

TILE = 512
BLK = 7
BAND = 14
SLOTS = 10
SCANS = 384

ROWS = BAND * TILE
HALF = ROWS // 2
ROW_LEN = (1152, 1152, 1280)
COLS = BLK * SCANS
COL_LEN = (512, 512, 384, 512, 384, 384)
SPLIT = 4
CHUNKS = BLK * SPLIT
CH = SCANS // SPLIT


def bases(lengths):
    out, at = [], 0
    for n in lengths:
        out.append(at)
        at += n
    return out


ROW_BASE = bases(ROW_LEN)
COL_BASE = bases(COL_LEN)
ROW_FIN = bases([n // 8 for n in ROW_LEN])
COL_FIN = bases([n // 8 for n in COL_LEN])
RCH = len(ROW_LEN)
CCH = len(COL_LEN)


class Place:
    def __init__(self):
        self.row = lax.axis_index("row")
        self.col = lax.axis_index("col")
        self.yl = self.row // 4
        self.z = self.row % 4
        self.x = self.col // 4
        self.yh = (self.col // 2) % 2
        self.core = self.col % 2
        self.bits = {
            "xa": ((self.x + 1) // 2) % 2,
            "xb": self.x // 2,
            "yh": self.yh,
            "za": ((self.z + 1) // 2) % 2,
            "zb": self.z // 2,
            "yl": self.yl,
            "core": self.core,
        }

    def at(self, x=None, yh=None, core=None, yl=None, z=None):
        x = self.x if x is None else x
        yh = self.yh if yh is None else yh
        core = self.core if core is None else core
        yl = self.yl if yl is None else yl
        z = self.z if z is None else z
        return (yl * 4 + z, x * 4 + yh * 2 + core)

    def partner(self, dim):
        if dim == "core":
            return self.at(core=1 - self.core)
        if dim == "yh":
            return self.at(yh=1 - self.yh)
        if dim == "yl":
            return self.at(yl=1 - self.yl)
        if dim == "xa":
            return self.at(x=self.x + 1 - 2 * (self.x % 2))
        if dim == "xb":
            return self.at(x=(self.x + 3 + 2 * (self.x % 2)) % 4)
        if dim == "za":
            return self.at(z=self.z + 1 - 2 * (self.z % 2))
        return self.at(z=(self.z + 3 + 2 * (self.z % 2)) % 4)


ROW_ORDERS = (("xa", "xb", "yh"), ("xb", "yh", "xa"), ("yh", "xa", "xb"))
COL_ORDERS = (("za", "zb", "yl"), ("zb", "za", "yl")) * 3


def greet(place, dims):
    barrier = pltpu.get_barrier_semaphore()
    for dim in dims:
        pl.semaphore_signal(barrier, inc=1, device_id=place.partner(dim), device_id_type=MESH)
    pl.semaphore_wait(barrier, len(dims))


def segments(place, base, length, dims):
    out = []
    start, n = base, length
    for dim in dims:
        n = n // 2
        bit = place.bits[dim]
        keep = pl.multiple_of(start + bit * n, 16)
        send = pl.multiple_of(start + (1 - bit) * n, 16)
        out.append((keep, send, n))
        start = keep
    return out


def block_of(n):
    for blk in (128, 112, 96, 80, 64, 48, 32, 16):
        if n % blk == 0:
            return blk
    return n


def add_rows(dst, dst_at, one, one_at, two, two_at, n):
    blk = block_of(n)

    def body(i, carry):
        o = i * blk
        a = one[pl.ds(pl.multiple_of(one_at + o, 16), blk), :].astype(F32)
        b = two[pl.ds(pl.multiple_of(two_at + o, 16), blk), :].astype(F32)
        dst[pl.ds(pl.multiple_of(dst_at + o, 16), blk), :] = (a + b).astype(dst.dtype)
        return carry

    lax.fori_loop(0, n // blk, body, 0)


def partial_kernel(rows_s, cols_s, count_s, omega_h, series_h, band_h, row_ref, col_ref, omega_ref, series_ref, band_ref,
                   racc_ref, cacc_ref, rout_ref, cout_ref, isem, rsem, csem):
    count = count_s[0]

    def loads(s):
        at = pl.multiple_of(cols_s[s] * TILE, TILE)
        return (pltpu.make_async_copy(omega_h.at[s], omega_ref.at[s], isem.at[s, 0]),
                pltpu.make_async_copy(series_h.at[:, pl.ds(at, TILE)], series_ref.at[s], isem.at[s, 1]),
                pltpu.make_async_copy(band_h.at[rows_s[s]], band_ref.at[s], isem.at[s, 2]))

    def fetch(s, carry):
        for load in loads(s):
            load.start()
        return carry

    lax.fori_loop(0, count, fetch, 0)

    def row_out(i):
        return pltpu.make_async_copy(rout_ref.at[i], row_ref.at[i], rsem.at[i])

    def col_out(i):
        return pltpu.make_async_copy(cout_ref.at[i], col_ref.at[i], csem.at[i])

    def clear(ids, stage, out, blocks):
        def one(i, carry):
            held = False
            for k in range(SLOTS):
                held = jnp.logical_or(held, jnp.logical_and(k < count, ids[k] == i))

            @pl.when(jnp.logical_not(held))
            def _():
                stage[i] = jnp.zeros(stage.shape[1:], BF16)
                out(i).start()

            return carry

        lax.fori_loop(0, blocks, one, 0)

    clear(rows_s, rout_ref, row_out, BAND)
    clear(cols_s, cout_ref, col_out, BLK)

    def again(ids, t):
        seen, more = False, False
        for k in range(SLOTS):
            same = ids[k] == ids[t]
            seen = jnp.logical_or(seen, jnp.logical_and(k < t, same))
            more = jnp.logical_or(more, jnp.logical_and(jnp.logical_and(k > t, k < count), same))
        return seen, jnp.logical_not(more)

    def work(s, carry):
        for load in loads(s):
            load.wait()
        half = omega_ref[s].astype(BF16)
        panel = series_ref[s]
        row_again, row_last = again(rows_s, s)
        col_again, col_last = again(cols_s, s)
        term = lax.dot_general(half, panel, (((1,), (1,)), ((), ())), preferred_element_type=F32)

        @pl.when(row_again)
        def _():
            racc_ref[rows_s[s]] += term

        @pl.when(jnp.logical_not(row_again))
        def _():
            racc_ref[rows_s[s]] = term

        term2 = jnp.dot(band_ref[s], half, preferred_element_type=F32)

        @pl.when(col_again)
        def _():
            cacc_ref[cols_s[s]] += term2

        @pl.when(jnp.logical_not(col_again))
        def _():
            cacc_ref[cols_s[s]] = term2

        @pl.when(row_last)
        def _():
            rout_ref[rows_s[s]] = racc_ref[rows_s[s]].astype(BF16)
            row_out(rows_s[s]).start()

        @pl.when(col_last)
        def _():
            cout_ref[cols_s[s]] = cacc_ref[cols_s[s]].astype(BF16)
            col_out(cols_s[s]).start()

        return carry

    lax.fori_loop(0, count, work, 0)
    for i in range(BAND):
        row_out(i).wait()
    for i in range(BLK):
        col_out(i).wait()


def band_kernel(series, band, sbuf, ss_b, rs_b, ss_y, ss_s, rs_s, ls):
    place = Place()
    core = place.core
    xs = place.yl * 2 + place.z // 2
    near = place.yh == place.z % 2
    source = jnp.logical_and(place.x == xs, near)
    sister = place.partner("core")
    over = place.partner("yh")
    dist = [(place.x - xs + 4) % 4, (xs - place.x + 4) % 4]
    onward = [place.at(x=(place.x + 1) % 4), place.at(x=(place.x + 3) % 4)]
    hops = [jnp.where(near, dist[s % 2], (dist[s % 2] + 4 - s // 2) % 4) for s in range(4)]
    lag = [jnp.where(near, 0, s // 2 + 1) + hops[s] + 1 - s // 2 for s in range(4)]
    crossing = [jnp.logical_and(near, dist[s % 2] == s // 2) for s in range(4)]

    def slot(i, which):
        return band.at[which * BLK + i // SPLIT, pl.ds(pl.multiple_of((i % SPLIT) * CH, 16), CH), :]

    def native(i, held):
        return held.at[pl.ds(pl.multiple_of((i % SPLIT) * CH, 16), CH),
                       pl.ds(pl.multiple_of((i // SPLIT) * TILE, TILE), TILE)]

    def to_next(src, i, s):
        return pltpu.make_async_remote_copy(src, slot(i, core), ss_b.at[i], rs_b.at[i],
                                            device_id=onward[s % 2], device_id_type=MESH)

    def to_over(src, i):
        return pltpu.make_async_remote_copy(src, slot(i, core), ss_y.at[i], rs_b.at[i],
                                            device_id=over, device_id_type=MESH)

    def to_sister(src, i):
        return pltpu.make_async_remote_copy(src, slot(i, core), ss_s.at[i], rs_s.at[i],
                                            device_id=sister, device_id_type=MESH)

    def keep_native(i):
        return pltpu.make_async_copy(native(i, sbuf), slot(i, core), ls.at[1 + i])

    load = pltpu.make_async_copy(series, sbuf, ls.at[0])

    @pl.when(source)
    def _():
        load.start()

    greet(place, ("core", "xa", "xb", "yh"))

    def forward(src, i, s):
        @pl.when(hops[s] < 3)
        def _():
            to_next(src, i, s).start()

        @pl.when(crossing[s])
        def _():
            to_over(src, i).start()

        to_sister(src, i).start()

    @pl.when(source)
    def _():
        def emit(k, carry):
            for s in (2, 3):
                forward(native(k * 4 + s, series), k * 4 + s, s)

            @pl.when(k > 0)
            def _():
                for s in (0, 1):
                    i = (k - 1) * 4 + s
                    forward(native(i, series), i, s)

            return carry

        lax.fori_loop(0, CHUNKS // 4, emit, 0)
        for s in (0, 1):
            i = CHUNKS - 4 + s
            forward(native(i, series), i, s)
        load.wait()

        def hold(i, carry):
            keep_native(i).start()
            return carry

        lax.fori_loop(0, CHUNKS, hold, 0)

    @pl.when(jnp.logical_not(source))
    def _():
        def tick(t, carry):
            for s in (2, 3, 0, 1):
                k = t - lag[s]

                @pl.when(jnp.logical_and(k >= 0, k < CHUNKS // 4))
                def _():
                    i = k * 4 + s
                    to_next(slot(i, core), i, s).wait_recv()
                    forward(slot(i, core), i, s)

            return carry

        lax.fori_loop(0, CHUNKS // 4 + 5, tick, 0)

    def drain(k, carry):
        for s in range(4):
            i = k * 4 + s
            to_sister(slot(i, 1 - core), i).wait_recv()
            to_sister(slot(i, core), i).wait_send()

            @pl.when(hops[s] < 3)
            def _():
                to_next(slot(i, core), i, s).wait_send()

            @pl.when(crossing[s])
            def _():
                to_over(slot(i, core), i).wait_send()

            @pl.when(source)
            def _():
                keep_native(i).wait()

        return carry

    lax.fori_loop(0, CHUNKS // 4, drain, 0)


def sums_kernel(rowpart, colpart, rowhalf, colhalf, squares, racc, rcore, rrecv, rfin, cacc, crecv, cfin,
                ss_k, rs_k, ss_r, rs_r, ss_s, rs_s, ss_c, rs_c, ls):
    place = Place()
    core = place.core
    sister = place.partner("core")
    home = core * HALF
    away = (1 - core) * HALF

    rsegs = [segments(place, ROW_BASE[o], ROW_LEN[o], ROW_ORDERS[o]) for o in range(RCH)]
    csegs = [segments(place, COL_BASE[o], COL_LEN[o], COL_ORDERS[o]) for o in range(CCH)]

    def landing(segs):
        out, at = [], 0
        for line in segs:
            row = []
            for keep, send, n in line:
                row.append(at)
                at += n
            out.append(row)
        return out

    rland = landing(rsegs)
    cland = landing(csegs)

    def part_at(which, o):
        return rowpart.at[pl.ds(pl.multiple_of(which + ROW_BASE[o], 16), ROW_LEN[o])]

    def pair(o):
        at = pl.ds(ROW_BASE[o], ROW_LEN[o])
        return pltpu.make_async_remote_copy(part_at(away, o), rcore.at[at], ss_k.at[o], rs_k.at[o],
                                            device_id=sister, device_id_type=MESH)

    def row_load(o):
        at = pl.ds(ROW_BASE[o], ROW_LEN[o])
        return pltpu.make_async_copy(part_at(home, o), racc.at[at], ls.at[o])

    def col_load(o):
        keep, send, n = csegs[o][0]
        return pltpu.make_async_copy(colpart.at[pl.ds(keep, n)], cacc.at[pl.ds(keep, n)], ls.at[RCH + o])

    def row_send(o, j):
        keep, send, n = rsegs[o][j]
        return pltpu.make_async_remote_copy(
            racc.at[pl.ds(send, n)], rrecv.at[pl.ds(rland[o][j], n)], ss_r.at[o * 6 + j], rs_r.at[o * 6 + j],
            device_id=place.partner(ROW_ORDERS[o][j]), device_id_type=MESH)

    def col_send(o, j):
        keep, send, n = csegs[o][j]
        src = colpart if j == 0 else cacc
        return pltpu.make_async_remote_copy(
            src.at[pl.ds(send, n)], crecv.at[pl.ds(cland[o][j], n)], ss_c.at[o * 6 + j], rs_c.at[o * 6 + j],
            device_id=place.partner(COL_ORDERS[o][j]), device_id_type=MESH)

    def row_at(start, n):
        return rowhalf.at[pl.ds(pl.multiple_of(home + start, 16), n)]

    def row_gather(o, j):
        keep, send, n = rsegs[o][j]
        src = rfin.at[pl.ds(ROW_FIN[o], n)] if j == 2 else row_at(keep, n)
        return pltpu.make_async_remote_copy(
            src, row_at(keep, n), ss_r.at[o * 6 + 3 + j], rs_r.at[o * 6 + 3 + j],
            device_id=place.partner(ROW_ORDERS[o][j]), device_id_type=MESH)

    def row_local(o):
        keep, send, n = rsegs[o][2]
        return pltpu.make_async_copy(rfin.at[pl.ds(ROW_FIN[o], n)], row_at(keep, n), ls.at[RCH + CCH + o])

    def row_share(o, j):
        if j == 3:
            keep, send, n = rsegs[o][2]
            src, start = rfin.at[pl.ds(ROW_FIN[o], n)], keep
        else:
            keep, send, n = rsegs[o][j]
            src, start = row_at(send, n), send
        return pltpu.make_async_remote_copy(
            src, row_at(start, n), ss_s.at[o * 4 + j], rs_s.at[o * 4 + j], device_id=sister, device_id_type=MESH)

    def col_at(start, n):
        return colhalf.at[pl.ds(start, n)]

    def col_gather(o, j):
        keep, send, n = csegs[o][j]
        src = cfin.at[pl.ds(COL_FIN[o], n)] if j == 2 else col_at(keep, n)
        return pltpu.make_async_remote_copy(
            src, col_at(keep, n), ss_c.at[o * 6 + 3 + j], rs_c.at[o * 6 + 3 + j],
            device_id=place.partner(COL_ORDERS[o][j]), device_id_type=MESH)

    def col_local(o):
        keep, send, n = csegs[o][2]
        return pltpu.make_async_copy(cfin.at[pl.ds(COL_FIN[o], n)], col_at(keep, n), ls.at[2 * RCH + CCH + o])

    for o in range(RCH):
        row_load(o).start()
    for o in range(CCH):
        col_load(o).start()
    greet(place, ("core", "xa", "xb", "yh", "za", "zb", "yl"))
    for o in range(RCH):
        pair(o).start()
    for o in range(CCH):
        col_send(o, 0).start()
    for o in range(RCH):
        row_load(o).wait()
        pair(o).wait_recv()
        add_rows(racc, ROW_BASE[o], racc, ROW_BASE[o], rcore, ROW_BASE[o], ROW_LEN[o])
        row_send(o, 0).start()

    def col_add(o, j):
        keep, send, n = csegs[o][j]
        if j == 0:
            col_load(o).wait()
        col_send(o, j).wait_recv()
        if j < 2:
            add_rows(cacc, keep, cacc, keep, crecv, cland[o][j], n)
            col_send(o, j + 1).start()
        else:
            add_rows(cfin, COL_FIN[o], cacc, keep, crecv, cland[o][j], n)
            col_gather(o, 2).start()
            col_local(o).start()

    def row_add(o, j, total):
        keep, send, n = rsegs[o][j]
        row_send(o, j).wait_recv()
        if j < 2:
            add_rows(racc, keep, racc, keep, rrecv, rland[o][j], n)
            row_send(o, j + 1).start()
            return total

        def body(i, total):
            a = racc[pl.ds(pl.multiple_of(keep + i * 16, 16), 16), :].astype(F32)
            b = rrecv[pl.ds(pl.multiple_of(rland[o][2] + i * 16, 16), 16), :].astype(F32)
            c = a + b
            rfin[pl.ds(pl.multiple_of(ROW_FIN[o] + i * 16, 16), 16), :] = c.astype(BF16)
            c2 = c * c
            return total + c2[:8] + c2[8:]

        total = lax.fori_loop(0, n // 16, body, total)
        row_gather(o, 2).start()
        row_local(o).start()
        row_share(o, 3).start()
        return total

    total = jnp.zeros((8, SCANS), F32)
    for j in range(3):
        for o in range(max(RCH, CCH)):
            if o < CCH:
                col_add(o, j)
            if o < RCH:
                total = row_add(o, j, total)
    squares[...] = total

    def col_pass(o, j):
        if j == 2:
            col_local(o).wait()
        col_gather(o, j).wait_recv()
        if j > 0:
            col_gather(o, j - 1).start()

    def row_pass(o, j):
        if j == 2:
            row_local(o).wait()
        row_gather(o, j).wait_recv()
        if j > 0:
            row_gather(o, j - 1).start()
        row_share(o, j).start()

    for j in (2, 1, 0):
        for o in range(max(RCH, CCH)):
            if o < CCH:
                col_pass(o, j)
            if o < RCH:
                row_pass(o, j)
    for o in range(RCH):
        pair(o).wait_send()
        for j in range(4):
            row_share(o, j).wait_recv()
            row_share(o, j).wait_send()
        for j in range(3):
            row_send(o, j).wait_send()
            row_gather(o, j).wait_send()
    for o in range(CCH):
        for j in range(3):
            col_send(o, j).wait_send()
            col_gather(o, j).wait_send()


def update_kernel(rows_s, cols_s, count_s, omega_h, rowhalf_h, band_h, series_h, colhalf_h, out_h, sums_ref,
                  omega_ref, rowhalf_ref, band_ref, series_ref, colhalf_ref, out_ref, zero_ref,
                  grad_ref, acc_ref, diag_ref, isem, osem):
    count = count_s[0]
    row_base = lax.axis_index("row") * BAND
    col_base = lax.axis_index("col") * BLK

    def loads(s):
        at = pl.multiple_of(cols_s[s] * TILE, TILE)
        return (pltpu.make_async_copy(omega_h.at[s], omega_ref.at[s], isem.at[s, 0]),
                pltpu.make_async_copy(rowhalf_h.at[rows_s[s]], rowhalf_ref.at[s], isem.at[s, 1]),
                pltpu.make_async_copy(band_h.at[rows_s[s]], band_ref.at[s], isem.at[s, 2]),
                pltpu.make_async_copy(series_h.at[:, pl.ds(at, TILE)], series_ref.at[s], isem.at[s, 3]),
                pltpu.make_async_copy(colhalf_h.at[cols_s[s]], colhalf_ref.at[s], isem.at[s, 4]))

    def store(s):
        return pltpu.make_async_copy(out_ref.at[s], out_h.at[s], osem.at[s])

    def store_zero(s):
        return pltpu.make_async_copy(zero_ref, out_h.at[s], osem.at[s])

    def fetch(s, carry):
        for load in loads(s):
            load.start()
        return carry

    lax.fori_loop(0, count, fetch, 0)
    zero_ref[...] = jnp.zeros_like(zero_ref)
    acc_ref[...] = jnp.zeros_like(acc_ref)
    diag_ref[...] = jnp.zeros_like(diag_ref)

    def clear(s, carry):
        store_zero(s).start()
        return carry

    lax.fori_loop(count, SLOTS, clear, 0)

    def work(s, carry):
        for load in loads(s):
            load.wait()
        panel = series_ref[s]
        sums = colhalf_ref[s]
        blk = 128

        def fold(v):
            return jnp.sum(v.reshape(blk // 8, 8, TILE), axis=0)

        before, model, after = acc_ref[0], acc_ref[1], acc_ref[2]
        for i in range(TILE // blk):
            at = slice(i * blk, (i + 1) * blk)
            grad = (0.5 / SCANS) * (
                jnp.dot(rowhalf_ref[s, at, :], panel, preferred_element_type=F32)
                + lax.dot_general(band_ref[s, :, at], sums, (((0,), (0,)), ((), ())), preferred_element_type=F32)
            )
            now = omega_ref[s, at, :]
            grad_ref[at, :] = grad
            stepped = now - STEP * grad
            updated = stepped - jnp.clip(stepped, -THRESH, THRESH)
            change = updated - now
            out_ref[s, at, :] = updated
            before += fold(jnp.abs(now))
            model += fold(change * (grad + change * (0.5 / STEP)))
            after += fold(jnp.abs(updated))
        acc_ref[0] = before
        acc_ref[1] = model
        acc_ref[2] = after

        @pl.when(row_base + rows_s[s] == col_base + cols_s[s])
        def _():
            mask = lax.broadcasted_iota(jnp.int32, (128, 128), 0) == lax.broadcasted_iota(jnp.int32, (128, 128), 1)
            for q in range(TILE // 128):
                at = slice(q * 128, (q + 1) * 128)

                def pick(v):
                    return jnp.sum(jnp.where(mask, v, 0.0), axis=0, keepdims=True)

                now = pick(omega_ref[s, at, at])
                plain = pick(grad_ref[at, at])
                shrunk = out_ref[s, at, at]
                old = pick(shrunk)
                grad = plain - 1.0 / now
                stepped = now - STEP * grad
                change = stepped - now
                old_change = old - now
                out_ref[s, at, at] = jnp.where(mask, stepped, shrunk)
                diag_ref[0:1] += jnp.log(now)
                diag_ref[1:2] -= jnp.abs(now)
                diag_ref[2:3] += (change * (grad + change * (0.5 / STEP))
                                  - old_change * (plain + old_change * (0.5 / STEP)))
                diag_ref[3:4] -= jnp.abs(old)

        store(s).start()
        return carry

    lax.fori_loop(0, count, work, 0)
    sums_ref[0:1] = diag_ref[0:1]
    for t in range(3):
        v = acc_ref[t]
        v = v[:, 0:128] + v[:, 128:256] + v[:, 256:384] + v[:, 384:512]
        sums_ref[1 + t:2 + t] = jnp.sum(v, axis=0, keepdims=True) + diag_ref[1 + t:2 + t]
    sums_ref[4:8] = jnp.zeros((4, 128), F32)

    def done(s, carry):
        store(s).wait()
        return carry

    def cleared(s, carry):
        store_zero(s).wait()
        return carry

    lax.fori_loop(0, count, done, 0)
    lax.fori_loop(count, SLOTS, cleared, 0)


def total_kernel(sums, squares, out, vec, recv_a, recv_b, ss, rs):
    place = Place()
    row, col = place.row, place.col
    barrier = pltpu.get_barrier_semaphore()
    for k in range(1, 16):
        pl.semaphore_signal(barrier, inc=1, device_id=(row, (col + k) % 16), device_id_type=MESH)
    for k in range(1, 8):
        pl.semaphore_signal(barrier, inc=1, device_id=((row + k) % 8, col), device_id_type=MESH)
    v = squares[...]
    v = jnp.sum(v, axis=0, keepdims=True)
    v = v[:, 0:128] + v[:, 128:256] + v[:, 256:384]
    spot = lax.broadcasted_iota(jnp.int32, (8, 128), 0) == 5
    vec[0] = sums[...] + jnp.where(spot, jnp.broadcast_to(v, (8, 128)), 0.0)
    pl.semaphore_wait(barrier, 22)

    def across(k):
        return pltpu.make_async_remote_copy(vec.at[0], recv_a.at[col], ss.at[k - 1], rs.at[k - 1],
                                            device_id=(row, (col + k) % 16), device_id_type=MESH)

    def down(k):
        return pltpu.make_async_remote_copy(vec.at[1], recv_b.at[row], ss.at[14 + k], rs.at[14 + k],
                                            device_id=((row + k) % 8, col), device_id_type=MESH)

    for k in range(1, 16):
        across(k).start()
    recv_a[col] = vec[0]
    for k in range(1, 16):
        across(k).wait_recv()
    total = recv_a[0]
    for k in range(1, 16):
        total = total + recv_a[k]
    vec[1] = total
    for k in range(1, 8):
        down(k).start()
    recv_b[row] = total
    for k in range(1, 8):
        down(k).wait_recv()
    total = recv_b[0]
    for k in range(1, 8):
        total = total + recv_b[k]
    s = jnp.sum(total, axis=1, keepdims=True)
    smooth = -s[0:1] + s[5:6] / (2.0 * SCANS)
    objective = smooth + PENALTY * s[1:2]
    bound = smooth + s[2:3] + PENALTY * s[3:4]
    out[0] = objective[0, 0]
    out[1] = bound[0, 0]
    for k in range(1, 16):
        across(k).wait_send()
    for k in range(1, 8):
        down(k).wait_send()


def plain(**kw):
    return pltpu.CompilerParams(vmem_limit_bytes=60 << 20, **kw)


dma = pltpu.SemaphoreType.DMA
VMEM = pl.BlockSpec(memory_space=pltpu.VMEM)
HBM = pl.BlockSpec(memory_space=pl.ANY)


def band_call(series, cid):
    return pl.pallas_call(
        band_kernel,
        out_shape=jax.ShapeDtypeStruct((BAND, SCANS, TILE), BF16),
        in_specs=[HBM], out_specs=HBM,
        scratch_shapes=[pltpu.VMEM((SCANS, BLK * TILE), BF16),
                        dma((CHUNKS,)), dma((CHUNKS,)), dma((CHUNKS,)), dma((CHUNKS,)), dma((CHUNKS,)),
                        dma((CHUNKS + 1,))],
        compiler_params=plain(collective_id=cid, has_side_effects=True), name="band",
    )(series)


def sums_call(row_part, col_part, cid):
    return pl.pallas_call(
        sums_kernel,
        out_shape=(jax.ShapeDtypeStruct((ROWS, SCANS), BF16), jax.ShapeDtypeStruct((COLS, TILE), BF16),
                   jax.ShapeDtypeStruct((8, SCANS), F32)),
        in_specs=[HBM, HBM], out_specs=(HBM, HBM, VMEM),
        scratch_shapes=[pltpu.VMEM((HALF, SCANS), BF16), pltpu.VMEM((HALF, SCANS), BF16),
                        pltpu.VMEM((HALF * 7 // 8, SCANS), BF16), pltpu.VMEM((HALF // 8, SCANS), BF16),
                        pltpu.VMEM((COLS, TILE), BF16), pltpu.VMEM((COLS * 7 // 8, TILE), BF16),
                        pltpu.VMEM((COLS // 8, TILE), BF16),
                        dma((RCH,)), dma((RCH,)), dma((6 * RCH,)), dma((6 * RCH,)),
                        dma((4 * RCH,)), dma((4 * RCH,)), dma((6 * CCH,)), dma((6 * CCH,)),
                        dma((2 * RCH + 2 * CCH,))],
        compiler_params=plain(collective_id=cid, has_side_effects=True), name="sums",
    )(row_part, col_part)


def partials_call(rows_s, cols_s, count, omega, series, band):
    return pl.pallas_call(
        partial_kernel,
        out_shape=(jax.ShapeDtypeStruct((BAND, TILE, SCANS), BF16), jax.ShapeDtypeStruct((BLK, SCANS, TILE), BF16)),
        grid_spec=pltpu.PrefetchScalarGridSpec(
            num_scalar_prefetch=3, grid=(),
            in_specs=[HBM, HBM, HBM],
            out_specs=(HBM, HBM),
            scratch_shapes=[pltpu.VMEM((SLOTS, TILE, TILE), F32), pltpu.VMEM((SLOTS, SCANS, TILE), BF16),
                            pltpu.VMEM((SLOTS, SCANS, TILE), BF16),
                            pltpu.VMEM((BAND, TILE, SCANS), F32), pltpu.VMEM((BLK, SCANS, TILE), F32),
                            pltpu.VMEM((BAND, TILE, SCANS), BF16), pltpu.VMEM((BLK, SCANS, TILE), BF16),
                            dma((SLOTS, 3)), dma((BAND,)), dma((BLK,))]),
        compiler_params=plain(), name="partials",
    )(rows_s, cols_s, count, omega, series, band)


def update_call(rows_s, cols_s, count, omega, row_half, band, series, col_half):
    return pl.pallas_call(
        update_kernel,
        out_shape=(jax.ShapeDtypeStruct((SLOTS, TILE, TILE), F32), jax.ShapeDtypeStruct((8, 128), F32)),
        grid_spec=pltpu.PrefetchScalarGridSpec(
            num_scalar_prefetch=3, grid=(),
            in_specs=[HBM, HBM, HBM, HBM, HBM],
            out_specs=(HBM, VMEM),
            scratch_shapes=[pltpu.VMEM((SLOTS, TILE, TILE), F32), pltpu.VMEM((SLOTS, TILE, SCANS), BF16),
                            pltpu.VMEM((SLOTS, SCANS, TILE), BF16), pltpu.VMEM((SLOTS, SCANS, TILE), BF16),
                            pltpu.VMEM((SLOTS, SCANS, TILE), BF16), pltpu.VMEM((SLOTS, TILE, TILE), F32),
                            pltpu.VMEM((TILE, TILE), F32),
                            pltpu.VMEM((TILE, TILE), F32), pltpu.VMEM((3, 8, TILE), F32), pltpu.VMEM((8, 128), F32),
                            dma((SLOTS, 5)), dma((SLOTS,))]),
        compiler_params=plain(), name="update",
    )(rows_s, cols_s, count, omega, row_half.reshape(BAND, TILE, SCANS), band, series, col_half.reshape(BLK, SCANS, TILE))


def local(series, omega_tiles, tile_row, tile_col, tile_count):
    omega = omega_tiles[0, 0]
    rows_s = tile_row[0, 0]
    cols_s = tile_col[0, 0]
    count = tile_count[0]
    band = band_call(series, 0)
    row_part, col_part = partials_call(rows_s, cols_s, count, omega, series, band)
    row_half, col_half, squares = sums_call(row_part.reshape(ROWS, SCANS), col_part.reshape(COLS, TILE), 1)
    omega_next, sums = update_call(rows_s, cols_s, count, omega, row_half, band, series, col_half)
    values = pl.pallas_call(
        total_kernel,
        out_shape=jax.ShapeDtypeStruct((2,), F32),
        in_specs=[VMEM, VMEM], out_specs=pl.BlockSpec(memory_space=pltpu.SMEM),
        scratch_shapes=[pltpu.VMEM((2, 8, 128), F32), pltpu.VMEM((16, 8, 128), F32), pltpu.VMEM((8, 8, 128), F32),
                        pltpu.SemaphoreType.DMA((22,)), pltpu.SemaphoreType.DMA((22,))],
        compiler_params=plain(collective_id=2, has_side_effects=True), name="total",
    )(sums, squares)
    return omega_next[None, None], values


def solution(mesh):
    placed = (
        P(None, "col"),
        P("row", "col", None, None, None),
        P("row", "col", None),
        P("row", "col", None),
        P("row", "col"),
    )
    return jax.shard_map(
        local,
        mesh=mesh,
        in_specs=placed,
        out_specs=(P("row", "col", None, None, None), P()),
        check_vma=False,
    )
```
